32 devices in a mesh: grid: 2 (over y), wide: 8 (over z, x), band: 2 (over core).
Axes of the slice: x: 2, y: 2, z: 4, core: 2. Of those that a mesh axis runs over, the one named last changes fastest.
Arguments:
- energy: float32 [1152, 32, 256], P(None, ('grid', 'wide'), 'band'), parts along dimension 1, may hold values from -6 to 6
- source_weights: bfloat16 [2, 1152, 1152], P(None, 'band'), may hold values from -0.1875 to 0.1875
- speed: float32 [1152], replicated, may hold values from 0.15 to 0.9
- direction: int32 [1152], replicated, may hold values from 0 to 35
- sea_mask: int32 [32, 256], P('grid', 'band'), parts along dimension 0, may hold values 0 or 1
Outputs:
- forecast: float32 [1152, 32, 256], P(None, ('grid', 'wide'), 'band'), parts along dimension 1
The draws below stay inside these ranges and needn't reach their ends.
There are 2 independent parts, one for each index of `grid`. The reference program is written for one: setup_inputs(seed, part) draws one part's arguments, and reference() takes and returns one part's arrays. A program takes and returns all parts, laid end to end along the dimension named above; an argument that names none is the same for every part. Nothing has to cross between parts.
Inputs may be any that keep to these rules, and one draw needn't show every extreme that they name: direction index of each bin, below 36.
All inputs are finite; a program needn't handle non-finite values. No bound on the sum of `sea_mask` on one device may be relied on, other than what follows from the above.
Results may differ from the reference program's by a relative error of at most 0.0011.
Values may be sent and summed in bfloat16 or wider, within the bound.
No kernel may reach another device: no remote copies, remote signals or barrier semaphores. Data moves between devices by JAX's collectives and lax.ppermute only.
A program may use at most 64 MiB of HBM per device.

```python
import math
import jax
import jax.numpy as jnp
from jax import lax

BINS = 1152
NDIR = 36
OUTER = 1
SUBSTEPS = 1
ROWS = 16
COLS = 256


def touch_ends(drawn, own_key, low, top_value):
    longest = drawn.shape.index(max(drawn.shape))
    spots = []
    for shift in (0, 1):
        where = [jax.random.randint(jax.random.fold_in(own_key, axis), (), 0, length) for axis, length in enumerate(drawn.shape)]
        where[longest] = (where[longest] + shift) % drawn.shape[longest]
        spots.append(tuple(where))
    return drawn.at[spots[0]].set(low).at[spots[1]].set(top_value)


def level_of(stream_key, dims, cuts, least, high):
    def one(position, shards_of):
        steps = jax.random.uniform(jax.random.fold_in(jax.random.fold_in(stream_key, 6), position), (shards_of,), jnp.float32, least / len(cuts), high / len(cuts))
        return jnp.repeat(jnp.exp(steps), dims[position] // shards_of).reshape((-1,) + (1,) * (len(dims) - position - 1))

    loudness = one(*cuts[0])
    for cut in cuts[1:]:
        loudness = loudness * one(*cut)
    return loudness


def bell_draw(own_key, shape, deviation, most, split=(), held_as=jnp.bfloat16):
    drawn = jax.random.normal(own_key, shape, jnp.float32) * deviation
    if len(split) > 0:
        drawn = level_of(own_key, shape, split, -0.22, 0.18) * drawn
    return jnp.clip(drawn, min=-most, max=most).astype(held_as)


def setup_inputs(seed: int = 0, part: int = 0) -> dict:
    key_list = jax.random.split(jax.random.key(seed), 6)
    part_keys = jax.random.split(jax.random.fold_in(key_list[5], part), 6)
    energy = bell_draw(part_keys[0], (BINS, ROWS, COLS), 1.0, 6.0, ((1, 8), (2, 2)), jnp.float32)
    source_weights = bell_draw(key_list[1], (2, BINS, BINS), BINS ** -0.5, 0.1875, ((1, 2),))
    speed = jnp.clip(jnp.exp(jax.random.uniform(key_list[2], (BINS,), jnp.float32, math.log(0.15), math.log(0.9))), 0.15, 0.9)
    direction = touch_ends(jax.random.randint(key_list[3], (BINS,), 0, NDIR), jax.random.fold_in(key_list[3], 1), 0, NDIR - 1).astype(jnp.int32)
    sea_mask = touch_ends((jax.random.randint(part_keys[4], (ROWS, COLS), 0, 4) < 3).astype(jnp.int32), jax.random.fold_in(part_keys[4], 1), 0, 1)
    return dict(energy=energy, source_weights=source_weights, speed=speed, direction=direction, sea_mask=sea_mask)


time_step = 0.5


def minmod_pair(first_value, second_value):
    return 0.5 * (jnp.sign(first_value) + jnp.sign(second_value)) * jnp.minimum(jnp.abs(first_value), jnp.abs(second_value))


def take_cells(values, begin_at, how_many, sweep_axis):
    return lax.slice_in_dim(values, begin_at, begin_at + how_many, axis=sweep_axis)


def sweep(padded, courant, sweep_axis):
    cell_count = padded.shape[sweep_axis] - 4
    face_count = cell_count + 1
    cell_diffs = jnp.diff(padded, axis=sweep_axis)
    face_diff = take_cells(cell_diffs, 1, face_count, sweep_axis)
    behind = take_cells(cell_diffs, 0, face_count, sweep_axis)
    ahead_diff = take_cells(cell_diffs, 2, face_count, sweep_axis)
    left_cell = take_cells(padded, 1, face_count, sweep_axis)
    right_cell = take_cells(padded, 2, face_count, sweep_axis)
    forward = courant >= 0.0
    upwind = jnp.where(forward, left_cell, right_cell)
    limit_diff = jnp.where(forward, behind, ahead_diff)
    speed_abs = jnp.abs(courant)
    face_flux = courant * upwind + 0.5 * speed_abs * (1.0 - speed_abs) * minmod_pair(face_diff, limit_diff)
    centre = take_cells(padded, 2, cell_count, sweep_axis)
    return centre - (take_cells(face_flux, 1, cell_count, sweep_axis) - take_cells(face_flux, 0, cell_count, sweep_axis))


def reference(energy, source_weights, speed, direction, sea_mask):
    sea_cells = sea_mask.astype(jnp.float32)
    angle_all = (direction.astype(jnp.float32) + 0.5) * (2.0 * math.pi / NDIR)
    row_courant = (speed * jnp.sin(angle_all))[:, None, None]
    col_courant = (speed * jnp.cos(angle_all))[:, None, None]
    field_now = energy
    for outer_step in range(OUTER):
        spectra = field_now.reshape(BINS, ROWS * COLS).astype(jnp.bfloat16)
        grow_term = jnp.dot(source_weights[0], spectra, preferred_element_type=jnp.float32)
        gate_term = jnp.dot(source_weights[1], spectra, preferred_element_type=jnp.float32)
        source_term = (grow_term * jax.nn.sigmoid(gate_term)).reshape(BINS, ROWS, COLS)
        field_now = field_now + time_step * source_term
        for sub_step in range(SUBSTEPS):
            padded = jnp.pad(field_now, ((0, 0), (2, 2), (0, 0)))
            field_now = sweep(padded, row_courant, 1)
            padded = jnp.pad(field_now, ((0, 0), (0, 0), (2, 2)))
            field_now = sweep(padded, col_courant, 2)
            field_now = field_now * sea_cells
    return field_now
```

```python
import functools
import math

import jax
import jax.numpy as jnp
from jax import lax
from jax.experimental import pallas as pl
from jax.experimental.pallas import tpu as pltpu
from jax.sharding import PartitionSpec as P

NDIR = 36
TIME_STEP = 0.5
F32 = jnp.float32
BF16 = jnp.bfloat16
VMEM = pl.BlockSpec(memory_space=pltpu.VMEM)
SMEM = pl.BlockSpec(memory_space=pltpu.SMEM)


def chunk_sizes(bins):
    tile = 128
    if bins % tile:
        return [bins]
    tiles = bins // tile
    first = (tiles + 1) // 2
    second = tiles - first
    return [n * tile for n in (first, second) if n]


def params(mib):
    return pltpu.CompilerParams(vmem_limit_bytes=mib * 1024 * 1024)


def prepare_kernel(energy, *parts):
    done = 0
    for part in parts:
        size = part.shape[1]
        for row in range(2):
            part[row] = energy[pl.ds(2 * done + row, size, stride=2), :].astype(BF16)
        done += size


def gather_points(parts, points):
    done = 0
    for part in parts:
        size = part.shape[1]
        for row in range(2):
            points[pl.ds(done, size), row * 128 : (row + 1) * 128] = part[row]
        done += size


def source(weights, rows, points):
    grow = jnp.dot(weights[0, rows, :], points[...], preferred_element_type=F32)
    gate = jnp.dot(weights[1, rows, :], points[...], preferred_element_type=F32)
    return TIME_STEP * (grow * jax.nn.sigmoid(gate))


def blocks(half):
    for size in (192, 96, 64, 32, 16):
        if half % size == 0:
            return size
    return half


def own_kernel(place, mine, other, energy, *refs):
    parts, field, points = refs[:-2], refs[-2], refs[-1]
    gather_points(parts, points)
    half = mine.shape[1]
    size = blocks(half)
    band = place[0]
    for weights, start in ((mine, band * half), (other, (1 - band) * half)):
        for k in range(0, half, size):
            src = source(weights, pl.ds(k, size), points)
            at = pl.multiple_of(start + k, 16)
            for row in range(2):
                mine_e = energy[pl.ds(2 * at + row, size, stride=2), :]
                field[row, pl.ds(at, size), :] = mine_e + src[:, row * 128 : (row + 1) * 128]


def halo_kernel(place, mine, other, *refs):
    parts, field, points = refs[:-2], refs[-2], refs[-1]
    gather_points(parts, points)
    half = mine.shape[1]
    size = blocks(half)
    band = place[0]
    for weights, start in ((mine, band * half), (other, (1 - band) * half)):
        for k in range(0, half, size):
            src = source(weights, pl.ds(k, size), points)
            at = pl.multiple_of(start + k, 16)
            for row in range(2):
                cells = slice(row * 128, (row + 1) * 128)
                field[row, pl.ds(at, size), :] = points[pl.ds(at, size), cells].astype(F32) + src[:, cells]


def limited(diff, other):
    return jnp.minimum(jnp.maximum(diff, jnp.minimum(other, 0.0)), jnp.maximum(other, 0.0))


def row_kernel(place, mine, other, courant, own, swapped, *refs):
    parts, field, edge, points, relayed = refs[:-4], refs[-4], refs[-3], refs[-2], refs[-1]
    gather_points(parts, points)
    half = mine.shape[1]
    size = blocks(half)
    band, odd = place[0], place[1] == 1
    for weights, start in ((mine, band * half), (other, (1 - band) * half)):
        for k in range(0, half, size):
            src = source(weights, pl.ds(k, size), points)
            at = pl.multiple_of(start + k, 16)
            for row in range(2):
                cells = slice(row * 128, (row + 1) * 128)
                relayed[row, pl.ds(at, size), :] = points[pl.ds(at, size), cells].astype(F32) + src[:, cells]
    step = 16
    lane = lax.broadcasted_iota(jnp.int32, (step, 128), 1)

    def body(i, _):
        at = pl.ds(pl.multiple_of(i * step, step), step)
        c = courant[at, :]
        forward = c >= 0.0
        a = jnp.abs(c)
        k = 0.5 * a * (1.0 - a)
        q0, q1 = own[0, at, :], own[1, at, :]
        s0, s1 = swapped[0, at, :], swapped[1, at, :]
        r0, r1 = relayed[0, at, :], relayed[1, at, :]
        up0, up1 = jnp.where(odd, s0, r0), jnp.where(odd, s1, r1)
        down0, down1 = jnp.where(odd, r0, s0), jnp.where(odd, r1, s1)
        m2 = jnp.where(forward, up0, down1)
        m1 = jnp.where(forward, up1, down0)
        c0 = jnp.where(forward, q0, q1)
        c1 = jnp.where(forward, q1, q0)
        p2 = jnp.where(forward, down0, up1)
        da, db, dc, dd = m1 - m2, c0 - m1, c1 - c0, p2 - c1
        fa = a * m1 + k * limited(db, da)
        fb = a * c0 + k * limited(dc, db)
        fc = a * c1 + k * limited(dd, dc)
        n0 = c0 - (fb - fa)
        n1 = c1 - (fc - fb)
        o0 = jnp.where(forward, n0, n1)
        o1 = jnp.where(forward, n1, n0)
        field[0, at, :] = o0
        field[1, at, :] = o1
        moved = jnp.where(lane < 64, pltpu.roll(o1, 2, axis=1), pltpu.roll(o1, 126, axis=1))
        outer = (lane < 2) | (lane >= 126)
        edge[at, :] = jnp.where(outer, o0, moved)
        return _

    lax.fori_loop(0, courant.shape[0] // step, body, 0, unroll=4)


def col_kernel(place, courant, mask, field, before, after, out):
    step = 16
    lane = lax.broadcasted_iota(jnp.int32, (step, 128), 1)
    first, last = lane == 0, lane == 127

    def body(i, _):
        at = pl.ds(pl.multiple_of(i * step, step), step)
        c = courant[at, :]
        forward = c >= 0.0
        a = jnp.abs(c)
        k = 0.5 * a * (1.0 - a)
        left, right = before[at, :], after[at, :]
        for row in range(2):
            q = field[row, at, :]
            l2 = jnp.broadcast_to(left[:, 126 - 2 * row : 127 - 2 * row], q.shape)
            l1 = jnp.broadcast_to(left[:, 127 - 2 * row : 128 - 2 * row], q.shape)
            r1 = jnp.broadcast_to(right[:, 2 * row : 2 * row + 1], q.shape)
            r2 = jnp.broadcast_to(right[:, 2 * row + 1 : 2 * row + 2], q.shape)
            ahead = jnp.where(last, r1, pltpu.roll(q, 127, axis=1))
            d = ahead - q
            dm = jnp.where(first, q - l1, pltpu.roll(d, 1, axis=1))
            dp = jnp.where(last, r2 - r1, pltpu.roll(d, 127, axis=1))
            flux = c * jnp.where(forward, q, ahead) + k * limited(d, jnp.where(forward, dm, dp))
            edge = c * jnp.where(forward, l1, q) + k * limited(q - l1, jnp.where(forward, l1 - l2, d))
            back = jnp.where(first, edge, pltpu.roll(flux, 1, axis=1))
            out[pl.ds(2 * i * step + row, step, stride=2), :] = (q - (flux - back)) * mask[row : row + 1, :]
        return _

    lax.fori_loop(0, courant.shape[0] // step, body, 0, unroll=4)


def local(energy, source_weights, speed, direction, sea_mask):
    bins, rows, cols = energy.shape
    wide, bands = lax.axis_size("wide"), lax.axis_size("band")
    w_at, b_at = lax.axis_index("wide"), lax.axis_index("band")
    flat = energy.reshape(bins * rows, cols)
    angle = (direction.astype(F32) + 0.5) * (2.0 * math.pi / NDIR)
    row_courant = jnp.broadcast_to((speed * jnp.sin(angle))[:, None], (bins, cols))
    col_courant = jnp.broadcast_to((speed * jnp.cos(angle))[:, None], (bins, cols))
    mask = lax.dynamic_slice_in_dim(sea_mask, w_at * rows, rows, 0).astype(F32)
    place = jnp.stack([b_at, w_at % 2]).astype(jnp.int32)

    sizes = chunk_sizes(bins)
    part_shapes = [jax.ShapeDtypeStruct((2, n, cols), BF16) for n in sizes]
    parts = pl.pallas_call(
        prepare_kernel, out_shape=part_shapes, in_specs=[VMEM], out_specs=[VMEM] * len(sizes),
        compiler_params=params(8), name="prepare",
    )(flat)
    swap = [(i, i ^ 1) for i in range(wide)]
    relay = [(i, i + 2) for i in range(0, wide - 2, 2)] + [(i, i - 2) for i in range(3, wide, 2)]
    swapped = [lax.ppermute(part, "wide", swap) for part in parts]
    other = lax.ppermute(source_weights, "band", [(i, i ^ 1) for i in range(bands)])
    relayed = [lax.ppermute(part, "wide", relay) for part in swapped]

    full = jax.ShapeDtypeStruct((2, bins, cols), F32)
    points = pltpu.VMEM((bins, 2 * cols), BF16)
    n = len(sizes)
    own = pl.pallas_call(
        own_kernel, out_shape=full, in_specs=[SMEM] + [VMEM] * (3 + n), out_specs=VMEM,
        scratch_shapes=[points], compiler_params=params(20), name="own",
    )(place, source_weights, other, flat, *parts)
    near = pl.pallas_call(
        halo_kernel, out_shape=full, in_specs=[SMEM] + [VMEM] * (2 + n), out_specs=VMEM,
        scratch_shapes=[points], compiler_params=params(20), name="near",
    )(place, source_weights, other, *swapped)
    field, edge = pl.pallas_call(
        row_kernel, out_shape=[full, jax.ShapeDtypeStruct((bins, cols), F32)],
        in_specs=[SMEM] + [VMEM] * (5 + n), out_specs=[VMEM, VMEM],
        scratch_shapes=[points, pltpu.VMEM((2, bins, cols), F32)],
        compiler_params=params(24), name="rows",
    )(place, source_weights, other, row_courant, own, near, *relayed)
    before = lax.ppermute(edge, "band", [(i, i + 1) for i in range(bands - 1)])
    after = lax.ppermute(edge, "band", [(i + 1, i) for i in range(bands - 1)])
    out = pl.pallas_call(
        col_kernel, out_shape=jax.ShapeDtypeStruct((bins * rows, cols), F32),
        in_specs=[SMEM] + [VMEM] * 5, out_specs=VMEM, compiler_params=params(20), name="cols",
    )(place, col_courant, mask, field, before, after)
    return out.reshape(bins, rows, cols)


def solution(mesh):
    return jax.shard_map(
        local,
        mesh=mesh,
        in_specs=(
            P(None, ("grid", "wide"), "band"),
            P(None, "band", None),
            P(),
            P(),
            P("grid", "band"),
        ),
        out_specs=P(None, ("grid", "wide"), "band"),
        check_vma=False,
    )
```

```python
import functools
import math

import jax
import jax.numpy as jnp
from jax import lax
from jax.experimental import pallas as pl
from jax.experimental.pallas import tpu as pltpu
from jax.sharding import PartitionSpec as P

NDIR = 36
TIME_STEP = 0.5
CHUNKS = 3
F32 = jnp.float32
BF16 = jnp.bfloat16
VMEM = pl.BlockSpec(memory_space=pltpu.VMEM)
SMEM = pl.BlockSpec(memory_space=pltpu.SMEM)
HBM = pl.BlockSpec(memory_space=pltpu.HBM)


def call(kernel, mib, **kw):
    return pl.pallas_call(
        kernel,
        compiler_params=pltpu.CompilerParams(vmem_limit_bytes=mib * 1024 * 1024), **kw,
    )


def chunk_sizes(bins):
    tile = 128 if bins % 128 == 0 else 16
    tiles = bins // tile
    cuts = [tiles * i // CHUNKS for i in range(CHUNKS + 1)]
    return [(b - a) * tile for a, b in zip(cuts, cuts[1:]) if b > a]


def prepare_kernel(start, energy, *refs):
    *parts, held, sems = refs
    piece = 128 if held.shape[0] % 256 == 0 else held.shape[0] // 2
    copies = []
    for i in range(held.shape[0] // (2 * piece)):
        copies.append(pltpu.make_async_copy(
            energy.at[pl.ds(2 * (start + i * piece), 2 * piece), :],
            held.at[pl.ds(2 * i * piece, 2 * piece), :], sems.at[i]))
        copies[-1].start()
    i = 0
    for part in parts:
        for k in range(0, part.shape[1], piece):
            copies[i].wait()
            for row in range(2):
                part[row, k : k + piece, :] = held[pl.ds(2 * i * piece + row, piece, stride=2), :].astype(BF16)
            i += 1


def gather_points(parts, points):
    done = 0
    for part in parts:
        size = part.shape[1]
        for row in range(2):
            points[pl.ds(done, size), row * 128 : (row + 1) * 128] = part[row]
        done += size


BLOCK = 192


def fetch(other, held, sem):
    copy = pltpu.make_async_copy(other, held, sem)
    copy.start()
    return copy


def sources(band, mine, held, copy, points):
    half = mine.shape[1]
    size = BLOCK if half % BLOCK == 0 else half
    for weights, start in ((mine, band * half), (held, (1 - band) * half)):
        if weights is held:
            copy.wait()
        for k in range(0, half, size):
            grow = jnp.dot(weights[0, k : k + size, :], points[...], preferred_element_type=F32)
            gate = jnp.dot(weights[1, k : k + size, :], points[...], preferred_element_type=F32)
            src = TIME_STEP * (grow * jax.nn.sigmoid(gate))
            yield pl.multiple_of(start + k, 16), size, src


def own_kernel(place, mine, other, energy, *refs):
    *parts, field, points, held, sem = refs
    copy = fetch(other, held, sem)
    gather_points(parts, points)
    for at, size, src in sources(place[0], mine, held, copy, points):
        for row in range(2):
            base = energy[pl.ds(2 * at + row, size, stride=2), :]
            field[row, pl.ds(at, size), :] = base + src[:, row * 128 : (row + 1) * 128]


def add_halo(points, field, at, size, src):
    for row in range(2):
        cells = slice(row * 128, (row + 1) * 128)
        field[row, pl.ds(at, size), :] = points[pl.ds(at, size), cells].astype(F32) + src[:, cells]


def near_kernel(place, mine, other, *refs):
    *parts, field, points, held, sem = refs
    copy = fetch(other, held, sem)
    gather_points(parts, points)
    for at, size, src in sources(place[0], mine, held, copy, points):
        add_halo(points, field, at, size, src)


def limited(a, b):
    return jnp.minimum(jnp.maximum(a, jnp.minimum(b, 0.0)), jnp.maximum(b, 0.0))


def row_kernel(place, mine, other, courants, _, own, near, *refs):
    *parts, field, edge, points, held, sem, far = refs
    copy = fetch(other, held, sem)
    gather_points(parts, points)
    for at, size, src in sources(place[0], mine, held, copy, points):
        add_halo(points, far, at, size, src)
    odd, inside = place[1] == 1, place[2] == 1
    shift = jnp.where(place[0] == 0, 1, 127)
    step = 16
    lane = lax.broadcasted_iota(jnp.int32, (step, 128), 1)
    outer = (lane == 0) | (lane == 127)

    def body(i, carry):
        at = pl.ds(pl.multiple_of(i * step, step), step)
        c = courants[0, at, :]
        forward = c >= 0.0
        a = jnp.abs(c)
        k = 0.5 * a * (1.0 - a)
        q0, q1 = own[0, at, :], own[1, at, :]
        s0, s1 = near[0, at, :], near[1, at, :]
        r0 = jnp.where(inside, far[0, at, :], 0.0)
        r1 = jnp.where(inside, far[1, at, :], 0.0)
        up0, up1 = jnp.where(odd, s0, r0), jnp.where(odd, s1, r1)
        down0, down1 = jnp.where(odd, r0, s0), jnp.where(odd, r1, s1)
        m2 = jnp.where(forward, up0, down1)
        m1 = jnp.where(forward, up1, down0)
        c0 = jnp.where(forward, q0, q1)
        c1 = jnp.where(forward, q1, q0)
        p2 = jnp.where(forward, down0, up1)
        da, db, dc, dd = m1 - m2, c0 - m1, c1 - c0, p2 - c1
        fa = a * m1 + k * limited(db, da)
        fb = a * c0 + k * limited(dc, db)
        fc = a * c1 + k * limited(dd, dc)
        n0 = c0 - (fb - fa)
        n1 = c1 - (fc - fb)
        o0 = jnp.where(forward, n0, n1)
        o1 = jnp.where(forward, n1, n0)
        field[0, at, :] = o0
        field[1, at, :] = o1
        edge[at, :] = jnp.where(outer, pltpu.roll(o0, shift, axis=1), pltpu.roll(o1, shift + 64 & 127, axis=1))
        return carry

    lax.fori_loop(0, courants.shape[1] // step, body, 0, unroll=4)


def col_kernel(place, courants, sea, field, beside, out, held, sems):
    step = 16
    lane = lax.broadcasted_iota(jnp.int32, (step, 128), 1)
    first, last = lane == 0, lane == 127
    outer = first | last
    left = place[0].astype(F32)
    right = 1.0 - left
    sign = right - left
    shift = jnp.where(place[0] == 1, 1, 127)
    bins = courants.shape[1]
    mask = [sea[pl.ds(place[3] + row, 1), :].astype(F32) for row in range(2)]
    piece = 128 if bins % 128 == 0 else bins

    def body(i, carry):
        at = pl.ds(pl.multiple_of(i * step, step), step)
        c = courants[1, at, :]
        forward = c >= 0.0
        a = jnp.abs(c)
        k = 0.5 * a * (1.0 - a)
        h1 = beside[at, :]
        h2 = pltpu.roll(h1, shift, axis=1)
        q0, q1 = field[0, at, :], field[1, at, :]
        ends = jnp.where(outer, q0, pltpu.roll(q1, 64, axis=1))
        ge = c * h1 + (sign * k) * limited(h1 - ends, h2 - h1)
        for row, q in ((0, q0), (1, q1)):
            h, e = (h1, ge) if row == 0 else (pltpu.roll(h1, 64, axis=1), pltpu.roll(ge, 64, axis=1))
            d = jnp.where(last, right * h, pltpu.roll(q, 127, axis=1)) - q
            dm = jnp.where(first, q - left * h, pltpu.roll(d, 1, axis=1))
            g = c * q + k * limited(d, dm)
            gm = jnp.where(first, left * e, pltpu.roll(g, 1, axis=1))
            gp = jnp.where(last, right * e, pltpu.roll(g, 127, axis=1))
            new = (q - jnp.where(forward, g - gm, gp - g)) * mask[row]
            held[pl.ds(2 * i * step + row, step, stride=2), :] = new
        return carry

    copies = []
    for j in range(bins // piece):
        lax.fori_loop(j * piece // step, (j + 1) * piece // step, body, 0, unroll=4)
        rows = pl.ds(2 * j * piece, 2 * piece)
        copies.append(pltpu.make_async_copy(held.at[rows, :], out.at[rows, :], sems.at[j]))
        copies[-1].start()
    for copy in copies:
        copy.wait()


def ring(count):
    order = list(range(0, count, 2)) + list(range(count - 1, 0, -2))
    return list(zip(order, order[1:] + order[:1]))


def local(energy, source_weights, speed, direction, sea_mask):
    bins, rows, cols = energy.shape
    wide, bands = lax.axis_size("wide"), lax.axis_size("band")
    if rows != 2 or cols != 128 or wide % 2 or bands != 2:
        raise ValueError("block shape")
    w_at, b_at = lax.axis_index("wide"), lax.axis_index("band")
    flat = energy.reshape(bins * rows, cols)
    sizes = chunk_sizes(bins)
    swap = [(i, i ^ 1) for i in range(wide)]
    beside = [(i, i ^ 1) for i in range(bands)]

    def prepare(start, these):
        total = sum(these)
        return call(
            functools.partial(prepare_kernel, start), 8,
            out_shape=[jax.ShapeDtypeStruct((2, n, cols), BF16) for n in these],
            in_specs=[HBM], out_specs=[VMEM] * len(these),
            scratch_shapes=[pltpu.VMEM((2 * total, cols), F32), pltpu.SemaphoreType.DMA((max(1, total // 128),))],
        )(pltpu.with_memory_space_constraint(flat, pltpu.HBM))

    other = lax.ppermute(source_weights, "band", beside)
    parts = prepare(0, sizes[:1])
    parts = parts + prepare(sizes[0], sizes[1:])
    swapped, relayed = [], []
    for part in parts:
        swapped.append(lax.ppermute(part, "wide", swap))
    for part in swapped:
        relayed.append(lax.ppermute(part, "wide", ring(wide)))

    angle = (direction.astype(F32) + 0.5) * (2.0 * math.pi / NDIR)
    courants = jnp.broadcast_to(
        jnp.stack([speed * jnp.sin(angle), speed * jnp.cos(angle)])[:, :, None], (2, bins, cols))
    inside = (w_at != 0) & (w_at != wide - 1)
    place = jnp.stack([b_at, w_at % 2, inside.astype(jnp.int32), w_at * rows]).astype(jnp.int32)

    full = jax.ShapeDtypeStruct((2, bins, cols), F32)
    scratch = [pltpu.VMEM((bins, 2 * cols), BF16), pltpu.VMEM(source_weights.shape, BF16), pltpu.SemaphoreType.DMA]
    other = pltpu.with_memory_space_constraint(other, pltpu.HBM)
    n = len(sizes)
    own = call(
        own_kernel, 8, out_shape=full, in_specs=[SMEM, VMEM, HBM] + [VMEM] * (1 + n),
        out_specs=VMEM, scratch_shapes=scratch,
    )(place, source_weights, other, flat, *parts)
    near = call(
        near_kernel, 8, out_shape=full, in_specs=[SMEM, VMEM, HBM] + [VMEM] * n,
        out_specs=VMEM, scratch_shapes=scratch,
    )(place, source_weights, other, *swapped)
    field, edge = call(
        row_kernel, 10, out_shape=[full, jax.ShapeDtypeStruct((bins, cols), F32)],
        in_specs=[SMEM, VMEM, HBM] + [VMEM] * (4 + n), out_specs=[VMEM, VMEM],
        scratch_shapes=scratch + [pltpu.VMEM((2, bins, cols), F32)],
    )(place, source_weights, other, courants, sea_mask, own, near, *relayed)
    edges = lax.ppermute(edge, "band", beside)
    out = call(
        col_kernel, 10, out_shape=jax.ShapeDtypeStruct((bins * rows, cols), F32),
        in_specs=[SMEM] + [VMEM] * 4, out_specs=HBM,
        scratch_shapes=[pltpu.VMEM((bins * rows, cols), F32), pltpu.SemaphoreType.DMA((max(1, bins // 128),))],
    )(place, courants, sea_mask, field, edges)
    return out.reshape(bins, rows, cols)


def solution(mesh):
    return jax.shard_map(
        local,
        mesh=mesh,
        in_specs=(
            P(None, ("grid", "wide"), "band"),
            P(None, "band", None),
            P(),
            P(),
            P("grid", "band"),
        ),
        out_specs=P(None, ("grid", "wide"), "band"),
        check_vma=False,
    )
```

```python
import functools
import math

import jax
import jax.numpy as jnp
from jax import lax
from jax.experimental import pallas as pl
from jax.experimental.pallas import tpu as pltpu
from jax.sharding import PartitionSpec as P

NDIR = 36
TIME_STEP = 0.5
CHUNKS = 3
GROUPS = 8
F32 = jnp.float32
BF16 = jnp.bfloat16
VMEM = pl.BlockSpec(memory_space=pltpu.VMEM)
SMEM = pl.BlockSpec(memory_space=pltpu.SMEM)
HBM = pl.BlockSpec(memory_space=pltpu.HBM)
ANY = pl.BlockSpec(memory_space=pl.ANY)


def call(kernel, mib, **kw):
    return pl.pallas_call(
        kernel,
        compiler_params=pltpu.CompilerParams(vmem_limit_bytes=mib * 1024 * 1024), **kw,
    )


def in_hbm(x):
    return pltpu.with_memory_space_constraint(x, pltpu.HBM)


def chunk_sizes(bins):
    tiles = bins // 128
    cuts = [tiles * i // CHUNKS for i in range(CHUNKS + 1)]
    return [(b - a) * 128 for a, b in zip(cuts, cuts[1:]) if b > a]


def prepare_kernel(energy, *refs):
    *parts, held, sems = refs
    piece = 128
    copies = []
    for i in range(held.shape[0] // (2 * piece)):
        at = pl.ds(2 * i * piece, 2 * piece)
        copies.append(pltpu.make_async_copy(energy.at[at, :], held.at[at, :], sems.at[i]))
        copies[-1].start()
    i = 0
    for part in parts:
        for k in range(0, part.shape[1], piece):
            copies[i].wait()
            for row in range(2):
                part[row, k : k + piece, :] = held[pl.ds(2 * i * piece + row, piece, stride=2), :].astype(BF16)
            i += 1


def gather_points(parts, points, start=0):
    for part in parts:
        size = part.shape[1]
        for row in range(2):
            points[pl.ds(start, size), row * 128 : (row + 1) * 128] = part[row]
        start += size


def blocks(band, mine, other, bins):
    size = bins // GROUPS
    half = mine.shape[1]
    for weights, start in ((mine, band * half), (other, (1 - band) * half)):
        for k in range(0, half, size):
            yield weights, slice(k, k + size), pl.multiple_of(start + k, 16)


def dots(weights, rows, points, first=0):
    part = slice(first, first + points.shape[0])
    return [jnp.dot(weights[i, rows, part], points[...], preferred_element_type=F32) for i in range(2)]


def gained(grow, gate):
    return TIME_STEP * (grow * jax.nn.sigmoid(gate))


def row_cells(row):
    return slice(row * 128, (row + 1) * 128)


def own_kernel(band_ref, mine, other, energy, courants, *refs):
    *parts, field, other_here, points, held, sems = refs
    bins = points.shape[0]
    size = bins // GROUPS
    copies = []
    for j, k in enumerate(range(0, mine.shape[1], size)):
        rows = pl.ds(k, size)
        copies.append(pltpu.make_async_copy(other.at[:, rows, :], other_here.at[:, rows, :], sems.at[j]))
    energy_copy = pltpu.make_async_copy(energy, held, sems.at[len(copies)])
    energy_copy.start()
    for copy in copies:
        copy.start()
    gather_points(parts, points)
    for n, (weights, rows, at) in enumerate(blocks(band_ref[0], mine, other_here, bins)):
        if n >= len(copies):
            copies[n - len(copies)].wait()
        src = gained(*dots(weights, rows, points))
        if n == 0:
            energy_copy.wait()
        for row in range(2):
            field[row, pl.ds(at, size), :] = held[pl.ds(2 * at + row, size, stride=2), :] + src[:, row_cells(row)]


def near_kernel(band_ref, mine, other, *refs):
    *parts, field, points = refs
    bins = points.shape[0]
    size = bins // GROUPS
    gather_points(parts, points)
    for weights, rows, at in blocks(band_ref[0], mine, other, bins):
        src = gained(*dots(weights, rows, points))
        for row in range(2):
            field[row, pl.ds(at, size), :] = points[pl.ds(at, size), row_cells(row)].astype(F32) + src[:, row_cells(row)]


def inside_points(wide_ref, last, parts, points, start=0):
    w = wide_ref[0]
    inside = (w != 0) & (w != last)

    @pl.when(inside)
    def _():
        gather_points(parts, points, start)

    @pl.when(jnp.logical_not(inside))
    def _():
        size = sum(part.shape[1] for part in parts)
        points[pl.ds(start, size), :] = jnp.zeros((size, points.shape[1]), points.dtype)


def partial_kernel(last, band_ref, wide_ref, mine, other, *refs):
    *parts, sums, points = refs
    bins = sums.shape[1]
    inside_points(wide_ref, last, parts, points)
    for weights, rows, at in blocks(band_ref[0], mine, other, bins):
        for i, value in enumerate(dots(weights, rows, points)):
            sums[i, pl.ds(at, value.shape[0]), :] = value


def limited(a, b):
    return jnp.minimum(jnp.maximum(a, jnp.minimum(b, 0.0)), jnp.maximum(b, 0.0))


def row_kernel(last, band_ref, wide_ref, mine, other, sums, courants, own, near, *refs):
    *parts, field, edge, points, far = refs
    bins = points.shape[0]
    first = bins - parts[-1].shape[1]
    size = bins // GROUPS
    band, odd = band_ref[0], lax.rem(wide_ref[0], 2)
    inside_points(wide_ref, last, parts, points)
    late = points.at[first:, :]
    shift = jnp.where(band == 0, 1, 127)
    lane = lax.broadcasted_iota(jnp.int32, (8, 128), 1)

    def sweep(weights, rows, at, behind, ahead, group, begin):
        mark = (lane - 2 * group) & 127
        mark0 = (mark == 0) | (mark == 127)
        mark1 = (mark == 64) | (mark == 63)
        shift0 = (shift + 2 * group) & 127
        shift1 = (shift0 + 64) & 127
        grow, gate = dots(weights, rows, late, first)
        src = gained(sums[0, pl.ds(at, size), :] + grow, sums[1, pl.ds(at, size), :] + gate)
        for row in range(2):
            base = points[pl.ds(at, size), row_cells(row)].astype(F32)
            far[row, pl.ds(at, size), :] = base + src[:, row_cells(row)]
        for i in range(0, size, 8):
            here = pl.ds(pl.multiple_of(at + i, 8), 8)
            c, k = courants[0, here, :], courants[1, here, :]
            forward = c >= 0.0
            a = jnp.abs(c)
            q0, q1 = own[0, here, :], own[1, here, :]
            m2 = jnp.where(forward, behind[0, here, :], ahead[1, here, :])
            m1 = jnp.where(forward, behind[1, here, :], ahead[0, here, :])
            c0 = jnp.where(forward, q0, q1)
            c1 = jnp.where(forward, q1, q0)
            p2 = jnp.where(forward, ahead[0, here, :], behind[1, here, :])
            da, db, dc, dd = m1 - m2, c0 - m1, c1 - c0, p2 - c1
            fa = a * m1 + k * limited(db, da)
            fb = a * c0 + k * limited(dc, db)
            fc = a * c1 + k * limited(dd, dc)
            n0 = c0 - (fb - fa)
            n1 = c1 - (fc - fb)
            o0 = jnp.where(forward, n0, n1)
            o1 = jnp.where(forward, n1, n0)
            field[0, here, :] = o0
            field[1, here, :] = o1
            before = jnp.zeros_like(o0) if begin else edge[i : i + 8, :]
            before = jnp.where(mark1, pltpu.roll(o1, shift1, axis=1), before)
            edge[i : i + 8, :] = jnp.where(mark0, pltpu.roll(o0, shift0, axis=1), before)

    def run(behind, ahead):
        for n, (weights, rows, at) in enumerate(blocks(band, mine, other, bins)):
            group = lax.rem(band * (GROUPS // 2) + n, GROUPS)
            sweep(weights, rows, at, behind, ahead, group, n == 0)

    @pl.when(odd == 1)
    def _():
        run(near, far)

    @pl.when(odd == 0)
    def _():
        run(far, near)


def col_kernel(band_ref, wide_ref, courants, sea, field, beside, out, held, sems):
    lane = lax.broadcasted_iota(jnp.int32, (8, 128), 1)
    first, last = lane == 0, lane == 127
    outer = first | last
    band = band_ref[0]
    left = band.astype(F32)
    right = 1.0 - left
    sign = right - left
    shift = jnp.where(band == 1, 1, 127)
    bins = courants.shape[1]
    size = bins // GROUPS
    place = 2 * wide_ref[0]
    mask = [jnp.broadcast_to(sea[pl.ds(place + row, 1), :].astype(F32), (8, 128)) for row in range(2)]
    shared = jnp.where(first, left, right) > 0.5

    def body(i, carry):
        i = pl.multiple_of(i * 8, 8)
        folded = beside[pl.ds(i, 8), :]
        for group in range(GROUPS):
            at = pl.multiple_of(group * size + i, 8)
            here = pl.ds(at, 8)
            c, k = courants[2, here, :], courants[3, here, :]
            forward = c >= 0.0
            a = jnp.abs(c)
            h1 = pltpu.roll(folded, (128 - 2 * group) & 127, axis=1) if group else folded
            h2 = pltpu.roll(folded, (shift + 128 - 2 * group) & 127, axis=1)
            q0, q1 = field[0, here, :], field[1, here, :]
            ends = jnp.where(outer, q0, pltpu.roll(q1, 64, axis=1))
            ge = a * h1 + (sign * k) * limited(h1 - ends, h2 - h1)
            ends_at = (first & forward) | (last & jnp.logical_not(forward))
            for row, q in ((0, q0), (1, q1)):
                h, e = (h1, ge) if row == 0 else (pltpu.roll(h1, 64, axis=1), pltpu.roll(ge, 64, axis=1))
                h = jnp.where(shared, h, 0.0)
                e = jnp.where(shared, e, 0.0)
                d = jnp.where(last, h, pltpu.roll(q, 127, axis=1)) - q
                dm = jnp.where(first, q - h, pltpu.roll(d, 1, axis=1))
                g = a * q + k * limited(d, dm)
                t = jnp.where(forward, pltpu.roll(g, 1, axis=1), pltpu.roll(g, 127, axis=1))
                t = jnp.where(ends_at, e, t)
                held[pl.ds(2 * at + row, 8, stride=2), :] = (q - (g - t)) * mask[row]
        return carry

    copies = []
    step = size // 3
    for part in range(3):
        lax.fori_loop(part * step // 8, (part + 1) * step // 8, body, 0)
        for group in range(GROUPS):
            rows = pl.ds(2 * (group * size + part * step), 2 * step)
            copies.append(pltpu.make_async_copy(held.at[rows, :], out.at[rows, :], sems.at[len(copies)]))
            copies[-1].start()
    for copy in copies:
        copy.wait()


def ring(count):
    order = list(range(0, count, 2)) + list(range(count - 1, 0, -2))
    return list(zip(order, order[1:] + order[:1]))


def local(energy, source_weights, speed, direction, sea_mask):
    bins, rows, cols = energy.shape
    wide, bands = lax.axis_size("wide"), lax.axis_size("band")
    if rows != 2 or cols != 128 or wide % 2 or bands != 2 or bins % (48 * GROUPS):
        raise ValueError("block shape")
    w_at = lax.axis_index("wide").astype(jnp.int32).reshape(1)
    b_at = lax.axis_index("band").astype(jnp.int32).reshape(1)
    flat = energy.reshape(bins * rows, cols)
    sizes = chunk_sizes(bins)
    swap = [(i, i ^ 1) for i in range(wide)]
    beside = [(i, i ^ 1) for i in range(bands)]

    other = lax.ppermute(source_weights, "band", beside)
    parts = call(
        prepare_kernel, 8,
        out_shape=[jax.ShapeDtypeStruct((2, n, cols), BF16) for n in sizes],
        in_specs=[HBM], out_specs=[VMEM] * len(sizes),
        scratch_shapes=[pltpu.VMEM((2 * bins, cols), F32), pltpu.SemaphoreType.DMA((bins // 128,))],
    )(in_hbm(flat))
    swapped, relayed = [], []
    for part in parts:
        swapped.append(lax.ppermute(part, "wide", swap))
    for part in swapped:
        relayed.append(lax.ppermute(part, "wide", ring(wide)))

    angle = (direction.astype(F32) + 0.5) * (2.0 * math.pi / NDIR)
    row_c, col_c = speed * jnp.sin(angle), speed * jnp.cos(angle)
    row_k, col_k = [0.5 * jnp.abs(c) * (1.0 - jnp.abs(c)) for c in (row_c, col_c)]
    table = jnp.stack([row_c, row_k, col_c, jnp.where(col_c >= 0.0, col_k, -col_k)])
    courants = jnp.broadcast_to(table[:, :, None], (4, bins, cols))

    full = jax.ShapeDtypeStruct((2, bins, cols), F32)
    sums = jax.ShapeDtypeStruct((2, bins, 2 * cols), F32)
    points = pltpu.VMEM((bins, 2 * cols), BF16)
    n = len(sizes)
    own, other = call(
        own_kernel, 8,
        out_shape=[full, jax.ShapeDtypeStruct(source_weights.shape, BF16)],
        in_specs=[SMEM, VMEM, HBM, HBM, ANY] + [VMEM] * n, out_specs=[VMEM, VMEM],
        scratch_shapes=[points, pltpu.VMEM((2 * bins, cols), F32), pltpu.SemaphoreType.DMA((GROUPS // 2 + 1,))],
    )(b_at, source_weights, in_hbm(other), in_hbm(flat), courants, *parts)
    near = call(
        near_kernel, 8, out_shape=full, in_specs=[SMEM] + [VMEM] * (2 + n),
        out_specs=VMEM, scratch_shapes=[points],
    )(b_at, source_weights, other, *swapped)
    early = call(
        functools.partial(partial_kernel, wide - 1), 8, out_shape=sums,
        in_specs=[SMEM, SMEM] + [VMEM] * (1 + n), out_specs=VMEM,
        scratch_shapes=[pltpu.VMEM((bins - sizes[-1], 2 * cols), BF16)],
    )(b_at, w_at, source_weights, other, *relayed[:-1])
    field, edge = call(
        functools.partial(row_kernel, wide - 1), 10,
        out_shape=[full, jax.ShapeDtypeStruct((bins // GROUPS, cols), F32)],
        in_specs=[SMEM, SMEM] + [VMEM] * (6 + n), out_specs=[VMEM, VMEM],
        scratch_shapes=[points, pltpu.VMEM((2, bins, cols), F32)],
    )(b_at, w_at, source_weights, other, early, courants, own, near, *relayed)
    edges = lax.ppermute(edge, "band", beside)
    out = call(
        col_kernel, 10, out_shape=jax.ShapeDtypeStruct((bins * rows, cols), F32),
        in_specs=[SMEM, SMEM] + [VMEM] * 4, out_specs=HBM,
        scratch_shapes=[pltpu.VMEM((bins * rows, cols), F32), pltpu.SemaphoreType.DMA((3 * GROUPS,))],
    )(b_at, w_at, courants, sea_mask, field, edges)
    return out.reshape(bins, rows, cols)


def solution(mesh):
    return jax.shard_map(
        local,
        mesh=mesh,
        in_specs=(
            P(None, ("grid", "wide"), "band"),
            P(None, "band", None),
            P(),
            P(),
            P("grid", "band"),
        ),
        out_specs=P(None, ("grid", "wide"), "band"),
        check_vma=False,
    )
```

```python
import functools
import math

import jax
import jax.numpy as jnp
from jax import lax
from jax.experimental import pallas as pl
from jax.experimental.pallas import tpu as pltpu
from jax.sharding import PartitionSpec as P

NDIR = 36
TIME_STEP = 0.5
CHUNKS = 3
GROUPS = 8
F32 = jnp.float32
BF16 = jnp.bfloat16
VMEM = pl.BlockSpec(memory_space=pltpu.VMEM)
SMEM = pl.BlockSpec(memory_space=pltpu.SMEM)
HBM = pl.BlockSpec(memory_space=pltpu.HBM)
ANY = pl.BlockSpec(memory_space=pl.ANY)


def call(kernel, mib, **kw):
    return pl.pallas_call(
        kernel,
        compiler_params=pltpu.CompilerParams(vmem_limit_bytes=mib * 1024 * 1024), **kw,
    )


def in_hbm(x):
    return pltpu.with_memory_space_constraint(x, pltpu.HBM)


def chunk_sizes(bins):
    tiles = bins // 128
    cuts = [tiles * i // CHUNKS for i in range(CHUNKS + 1)]
    return [(b - a) * 128 for a, b in zip(cuts, cuts[1:]) if b > a]


def prepare_kernel(energy, *refs):
    *parts, held, sems = refs
    piece = 128
    copies = []
    for i in range(held.shape[0] // (2 * piece)):
        at = pl.ds(2 * i * piece, 2 * piece)
        copies.append(pltpu.make_async_copy(energy.at[at, :], held.at[at, :], sems.at[i]))
        copies[-1].start()
    i = 0
    for part in parts:
        for k in range(0, part.shape[1], piece):
            copies[i].wait()
            for row in range(2):
                part[row, k : k + piece, :] = held[pl.ds(2 * i * piece + row, piece, stride=2), :].astype(BF16)
            i += 1


def gather_points(parts, points, start=0):
    for part in parts:
        size = part.shape[1]
        for row in range(2):
            points[pl.ds(start, size), row * 128 : (row + 1) * 128] = part[row]
        start += size


def blocks(band, mine, other, bins):
    size = bins // GROUPS
    half = bins // 2
    for j in range(GROUPS):
        weights, start = (mine, band * half) if j < GROUPS // 2 else (other, (1 - band) * half)
        k = j % (GROUPS // 2) * size
        yield j, weights, slice(k, k + size), pl.multiple_of(start + k, 16)


def dots(weights, rows, points, first=0):
    part = slice(first, first + points.shape[0])
    return [jnp.dot(weights[i, rows, part], points[...], preferred_element_type=F32) for i in range(2)]


def start_rows(source, target, sems, size):
    copies = []
    for j, k in enumerate(range(0, source.shape[1], size)):
        rows = pl.ds(k, size)
        copies.append(pltpu.make_async_copy(source.at[:, rows, :], target.at[:, rows, :], sems.at[j]))
        copies[-1].start()
    return copies


def gained(grow, gate):
    return TIME_STEP * (grow * jax.nn.sigmoid(gate))


def row_cells(row):
    return slice(row * 128, (row + 1) * 128)


def fill_tables(speed, direction, row_tables, col_tables):
    angle = (direction[...].astype(F32) + 0.5) * (2.0 * math.pi / NDIR)
    row_c, col_c = speed[...] * jnp.sin(angle), speed[...] * jnp.cos(angle)
    row_k, col_k = [0.5 * jnp.abs(c) * (1.0 - jnp.abs(c)) for c in (row_c, col_c)]
    col_k = jnp.where(col_c >= 0.0, col_k, -col_k)
    for tables, i, value in ((row_tables, 0, row_c), (row_tables, 1, row_k), (col_tables, 0, col_c), (col_tables, 1, col_k)):
        turned = value.T
        for r in range(value.shape[0]):
            tables[i, r * 128 : (r + 1) * 128, :] = jnp.broadcast_to(turned[:, r : r + 1], (128, 128))


def own_kernel(band_ref, mine, other, energy, out, points, held, here, field, energy_sems, in_sems, out_sems):
    bins = points.shape[0]
    size = bins // GROUPS
    energy_copies = []
    for i in range(bins // 128):
        at = pl.ds(256 * i, 256)
        energy_copies.append(pltpu.make_async_copy(energy.at[at, :], held.at[at, :], energy_sems.at[i]))
        energy_copies[-1].start()
    copies = start_rows(mine, here, in_sems, size)
    for i, copy in enumerate(energy_copies):
        copy.wait()
        for row in range(2):
            cells = held[pl.ds(256 * i + row, 128, stride=2), :].astype(BF16)
            points[128 * i : 128 * i + 128, row_cells(row)] = cells
    outs = []
    for j, weights, rows, at in blocks(band_ref[0], here, other, bins):
        if j < len(copies):
            copies[j].wait()
        src = gained(*dots(weights, rows, points))
        at = pl.ds(at, size)
        for row in range(2):
            field[row, at, :] = held[pl.ds(2 * at.start + row, size, stride=2), :] + src[:, row_cells(row)]
        outs.append(pltpu.make_async_copy(field.at[:, at, :], out.at[:, at, :], out_sems.at[j]))
        outs[-1].start()
    for copy in outs:
        copy.wait()


def near_kernel(band_ref, mine, other, own, speed, direction, *refs):
    *parts, field, here, own_here, row_tables, col_tables, points, in_sems, own_sem = refs
    bins = points.shape[0]
    size = bins // GROUPS
    copies = start_rows(mine, here, in_sems, size)
    own_copy = pltpu.make_async_copy(own, own_here, own_sem)
    own_copy.start()
    gather_points(parts, points)
    fill_tables(speed, direction, row_tables, col_tables)
    for j, weights, rows, at in blocks(band_ref[0], here, other, bins):
        if j < len(copies):
            copies[j].wait()
        src = gained(*dots(weights, rows, points))
        at = pl.ds(at, size)
        for row in range(2):
            field[row, at, :] = points[at, row_cells(row)].astype(F32) + src[:, row_cells(row)]
    own_copy.wait()


def inside_points(wide_ref, last, parts, points, start=0):
    w = wide_ref[0]
    inside = (w != 0) & (w != last)

    @pl.when(inside)
    def _():
        gather_points(parts, points, start)

    @pl.when(jnp.logical_not(inside))
    def _():
        size = sum(part.shape[1] for part in parts)
        points[pl.ds(start, size), :] = jnp.zeros((size, points.shape[1]), points.dtype)


def partial_kernel(last, band_ref, wide_ref, mine, other, *refs):
    *parts, sums, points = refs
    bins = sums.shape[1]
    inside_points(wide_ref, last, parts, points)
    for _, weights, rows, at in blocks(band_ref[0], mine, other, bins):
        for i, value in enumerate(dots(weights, rows, points)):
            sums[i, pl.ds(at, value.shape[0]), :] = value


def limited(a, b):
    return jnp.minimum(jnp.maximum(a, jnp.minimum(b, 0.0)), jnp.maximum(b, 0.0))


def row_kernel(last, band_ref, wide_ref, mine, other, sums, tables, own, near, *refs):
    *parts, field, edge, points, far = refs
    bins = points.shape[0]
    first = bins - parts[-1].shape[1]
    size = bins // GROUPS
    odd = lax.rem(wide_ref[0], 2)
    to_right = band_ref[0] == 0
    inside_points(wide_ref, last, parts, points)
    late = points.at[first:, :]
    lane = lax.broadcasted_iota(jnp.int32, (8, 128), 1)
    near_lane = jnp.where(to_right, 0, 127)
    near_roll = jnp.where(to_right, 1, 127)
    next_roll = jnp.where(to_right, 34, 30)

    def sweep(j, weights, rows, start, behind, ahead):
        group = lax.rem(band_ref[0] * (GROUPS // 2) + j, GROUPS)
        marks = [lane == ((near_lane + 2 * group + 32 * n) & 127) for n in range(4)]
        rolls = [(roll + 2 * group + 64 * row) & 127 for row in range(2) for roll in (near_roll, next_roll)]
        at = pl.ds(start, size)
        grow, gate = dots(weights, rows, late, first)
        src = gained(sums[0, at, :] + grow, sums[1, at, :] + gate)
        for row in range(2):
            far[row, at, :] = points[at, row_cells(row)].astype(F32) + src[:, row_cells(row)]
        for i in range(0, size, 8):
            here = pl.ds(pl.multiple_of(start + i, 8), 8)
            c, k = tables[0, here, :], tables[1, here, :]
            forward = c >= 0.0
            a = jnp.abs(c)
            q0, q1 = own[0, here, :], own[1, here, :]
            m2 = jnp.where(forward, behind[0, here, :], ahead[1, here, :])
            m1 = jnp.where(forward, behind[1, here, :], ahead[0, here, :])
            c0 = jnp.where(forward, q0, q1)
            c1 = jnp.where(forward, q1, q0)
            p2 = jnp.where(forward, ahead[0, here, :], behind[1, here, :])
            da, db, dc, dd = m1 - m2, c0 - m1, c1 - c0, p2 - c1
            fa = a * m1 + k * limited(db, da)
            fb = a * c0 + k * limited(dc, db)
            fc = a * c1 + k * limited(dd, dc)
            n0 = c0 - (fb - fa)
            n1 = c1 - (fc - fb)
            o0 = jnp.where(forward, n0, n1)
            o1 = jnp.where(forward, n1, n0)
            field[0, here, :] = o0
            field[1, here, :] = o1
            folded = edge[i : i + 8, :] if j else jnp.zeros_like(o0)
            for mark, roll, value in zip(marks, rolls, (o0, o0, o1, o1)):
                folded = jnp.where(mark, pltpu.roll(value, roll, axis=1), folded)
            edge[i : i + 8, :] = folded

    def run(behind, ahead):
        for j, weights, rows, start in blocks(band_ref[0], mine, other, bins):
            sweep(j, weights, rows, start, behind, ahead)

    @pl.when(odd == 1)
    def _():
        run(near, far)

    @pl.when(odd == 0)
    def _():
        run(far, near)


def col_kernel(band_ref, wide_ref, tables, sea, field, beside, out, held, sems):
    lane = lax.broadcasted_iota(jnp.int32, (8, 128), 1)
    first, last = lane == 0, lane == 127
    outer = first | last
    sign = (1 - 2 * band_ref[0]).astype(F32)
    bins = tables.shape[1]
    size = bins // GROUPS
    place = 2 * wide_ref[0]
    mask = [jnp.broadcast_to(sea[pl.ds(place + row, 1), :].astype(F32), (8, 128)) for row in range(2)]

    def cells(i, group):
        at = group * size + i
        here = slice(at, at + 8)
        c, k = tables[0, here, :], tables[1, here, :]
        forward = c >= 0.0
        a = jnp.abs(c)
        folded = beside[i : i + 8, :]
        h1 = pltpu.roll(folded, -2 * group % 128, axis=1) if group else folded
        h2 = pltpu.roll(folded, (-32 - 2 * group) % 128, axis=1)
        q0, q1 = field[0, here, :], field[1, here, :]
        ends = jnp.where(outer, q0, pltpu.roll(q1, 64, axis=1))
        ge = a * h1 + (sign * k) * limited(h1 - ends, h2 - h1)
        ends_at = (first & forward) | (last & jnp.logical_not(forward))
        for row, q in ((0, q0), (1, q1)):
            h, e = (h1, ge) if row == 0 else (pltpu.roll(h1, 64, axis=1), pltpu.roll(ge, 64, axis=1))
            d = jnp.where(last, h, pltpu.roll(q, 127, axis=1)) - q
            dm = jnp.where(first, q - h, pltpu.roll(d, 1, axis=1))
            g = a * q + k * limited(d, dm)
            t = jnp.where(forward, pltpu.roll(g, 1, axis=1), pltpu.roll(g, 127, axis=1))
            t = jnp.where(ends_at, e, t)
            held[pl.ds(2 * at + row, 8, stride=2), :] = (q - (g - t)) * mask[row]

    copies = []
    for group in range(GROUPS):
        for i in range(0, size, 8):
            cells(i, group)
        rows = pl.ds(2 * group * size, 2 * size)
        copies.append(pltpu.make_async_copy(held.at[rows, :], out.at[rows, :], sems.at[group]))
        copies[-1].start()
    for copy in copies:
        copy.wait()


def ring(count):
    order = list(range(0, count, 2)) + list(range(count - 1, 0, -2))
    return list(zip(order, order[1:] + order[:1]))


def local(energy, source_weights, speed, direction, sea_mask):
    bins, rows, cols = energy.shape
    wide, bands = lax.axis_size("wide"), lax.axis_size("band")
    if rows != 2 or cols != 128 or wide % 2 or bands != 2 or bins % (16 * GROUPS):
        raise ValueError("block shape")
    w_at = lax.axis_index("wide").astype(jnp.int32).reshape(1)
    b_at = lax.axis_index("band").astype(jnp.int32).reshape(1)
    flat = energy.reshape(bins * rows, cols)
    sizes = chunk_sizes(bins)
    swap = [(i, i ^ 1) for i in range(wide)]
    beside = [(i, i ^ 1) for i in range(bands)]

    other = lax.ppermute(source_weights, "band", beside)
    parts = call(
        prepare_kernel, 8,
        out_shape=[jax.ShapeDtypeStruct((2, n, cols), BF16) for n in sizes],
        in_specs=[HBM], out_specs=[VMEM] * len(sizes),
        scratch_shapes=[pltpu.VMEM((2 * bins, cols), F32), pltpu.SemaphoreType.DMA((bins // 128,))],
    )(in_hbm(flat))
    swapped, relayed = [], []
    for part in parts:
        swapped.append(lax.ppermute(part, "wide", swap))
    for part in swapped:
        relayed.append(lax.ppermute(part, "wide", ring(wide)))

    full = jax.ShapeDtypeStruct((2, bins, cols), F32)
    sums = jax.ShapeDtypeStruct((2, bins, 2 * cols), F32)
    points = pltpu.VMEM((bins, 2 * cols), BF16)
    n = len(sizes)
    table = jax.ShapeDtypeStruct((2, bins, cols), F32)
    half = jax.ShapeDtypeStruct(source_weights.shape, BF16)
    here = pltpu.VMEM(source_weights.shape, BF16)
    in_sems = pltpu.SemaphoreType.DMA((GROUPS // 2,))
    mine = in_hbm(source_weights)
    own = call(
        own_kernel, 9, out_shape=pltpu.HBM(full.shape, F32), in_specs=[SMEM, HBM, VMEM, HBM], out_specs=HBM,
        scratch_shapes=[points, pltpu.VMEM((2 * bins, cols), F32), here, pltpu.VMEM((2, bins, cols), F32),
                        pltpu.SemaphoreType.DMA((bins // 128,)), in_sems, pltpu.SemaphoreType.DMA((GROUPS,))],
    )(b_at, mine, other, in_hbm(flat))
    near, mine, own, row_tables, col_tables = call(
        near_kernel, 8, out_shape=[full, half, full, table, table],
        in_specs=[SMEM, HBM, VMEM, HBM] + [VMEM] * (2 + n), out_specs=[VMEM] * 5,
        scratch_shapes=[points, in_sems, pltpu.SemaphoreType.DMA],
    )(b_at, mine, other, in_hbm(own), speed.reshape(-1, 128), direction.reshape(-1, 128), *swapped)
    early = call(
        functools.partial(partial_kernel, wide - 1), 8, out_shape=sums,
        in_specs=[SMEM, SMEM] + [VMEM] * (1 + n), out_specs=VMEM,
        scratch_shapes=[pltpu.VMEM((bins - sizes[-1], 2 * cols), BF16)],
    )(b_at, w_at, mine, other, *relayed[:-1])
    field, edge = call(
        functools.partial(row_kernel, wide - 1), 10,
        out_shape=[full, jax.ShapeDtypeStruct((bins // GROUPS, cols), F32)],
        in_specs=[SMEM, SMEM] + [VMEM] * (6 + n), out_specs=[VMEM, VMEM],
        scratch_shapes=[points, pltpu.VMEM((2, bins, cols), F32)],
    )(b_at, w_at, mine, other, early, row_tables, own, near, *relayed)
    edges = lax.ppermute(edge, "band", beside)
    out = call(
        col_kernel, 10, out_shape=jax.ShapeDtypeStruct((bins * rows, cols), F32),
        in_specs=[SMEM, SMEM] + [VMEM] * 4, out_specs=HBM,
        scratch_shapes=[pltpu.VMEM((bins * rows, cols), F32), pltpu.SemaphoreType.DMA((GROUPS,))],
    )(b_at, w_at, col_tables, sea_mask, field, edges)
    return out.reshape(bins, rows, cols)


def solution(mesh):
    return jax.shard_map(
        local,
        mesh=mesh,
        in_specs=(
            P(None, ("grid", "wide"), "band"),
            P(None, "band", None),
            P(),
            P(),
            P("grid", "band"),
        ),
        out_specs=P(None, ("grid", "wide"), "band"),
        check_vma=False,
    )
```

```python
import functools
import math

import jax
import jax.numpy as jnp
from jax import lax
from jax.experimental import pallas as pl
from jax.experimental.pallas import tpu as pltpu
from jax.sharding import PartitionSpec as P

NDIR = 36
TIME_STEP = 0.5
CHUNKS = 2
GROUPS = 8
STEP = 16
F32 = jnp.float32
BF16 = jnp.bfloat16
VMEM = pl.BlockSpec(memory_space=pltpu.VMEM)
SMEM = pl.BlockSpec(memory_space=pltpu.SMEM)
HBM = pl.BlockSpec(memory_space=pltpu.HBM)
ANY = pl.BlockSpec(memory_space=pl.ANY)


def call(kernel, mib, **kw):
    return pl.pallas_call(
        kernel,
        compiler_params=pltpu.CompilerParams(vmem_limit_bytes=mib * 1024 * 1024), **kw,
    )


def in_hbm(x):
    return pltpu.with_memory_space_constraint(x, pltpu.HBM)


def chunk_sizes(bins):
    tiles = bins // 128
    cuts = [-(-tiles * i // CHUNKS) for i in range(CHUNKS + 1)]
    return [(b - a) * 128 for a, b in zip(cuts, cuts[1:]) if b > a]


def prepare_kernel(start, energy, *refs):
    *parts, held, sems = refs
    piece = 128
    copies = []
    for i in range(held.shape[0] // (2 * piece)):
        from_at, to_at = pl.ds(2 * (start + i * piece), 2 * piece), pl.ds(2 * i * piece, 2 * piece)
        copies.append(pltpu.make_async_copy(energy.at[from_at, :], held.at[to_at, :], sems.at[i]))
        copies[-1].start()
    i = 0
    for part in parts:
        for k in range(0, part.shape[1], piece):
            copies[i].wait()
            for row in range(2):
                part[row, k : k + piece, :] = held[pl.ds(2 * i * piece + row, piece, stride=2), :].astype(BF16)
            i += 1


def points_copies(parts, points, sems):
    copies, start = [], 0
    for part in parts:
        size = part.shape[1]
        for row in range(2):
            target = points.at[pl.ds(start, size), row * 128 : (row + 1) * 128]
            copies.append(pltpu.make_async_copy(part.at[row], target, sems.at[len(copies)]))
        start += size
    return copies


def gather_points(parts, points, start=0):
    for part in parts:
        size = part.shape[1]
        for row in range(2):
            points[pl.ds(start, size), row * 128 : (row + 1) * 128] = part[row]
        start += size


def blocks(band, mine, other, bins):
    size = bins // GROUPS
    half = bins // 2
    for j in range(GROUPS):
        weights, start = (other, (1 - band) * half) if j < GROUPS // 2 else (mine, band * half)
        k = j % (GROUPS // 2) * size
        yield j, weights, slice(k, k + size), pl.multiple_of(start + k, 16)


def dots(weights, rows, points, first=0):
    part = slice(first, first + points.shape[0])
    return [jnp.dot(weights[i, rows, part], points[...], preferred_element_type=F32) for i in range(2)]


def start_rows(source, target, sems, size):
    copies = []
    for j, k in enumerate(range(0, source.shape[1], size)):
        rows = pl.ds(k, size)
        copies.append(pltpu.make_async_copy(source.at[:, rows, :], target.at[:, rows, :], sems.at[j]))
        copies[-1].start()
    return copies


def gained(grow, gate):
    return TIME_STEP * (grow * jax.nn.sigmoid(gate))


def row_cells(row):
    return slice(row * 128, (row + 1) * 128)


def table_kernel(speed, direction, row_out, col_out, row_table, col_table, sems):
    angle = (direction[...].astype(F32) + 0.5) * (2.0 * math.pi / NDIR)
    copies = []
    for n, (out, table, c) in enumerate((
        (row_out, row_table, speed[...] * jnp.sin(angle)), (col_out, col_table, speed[...] * jnp.cos(angle)),
    )):
        turned = c.T
        for r in range(c.shape[0]):
            table[r * 128 : (r + 1) * 128, :] = jnp.broadcast_to(turned[:, r : r + 1], (128, 128))
        copies.append(pltpu.make_async_copy(table, out, sems.at[n]))
        copies[-1].start()
    for copy in copies:
        copy.wait()


def own_kernel(band_ref, mine, other, energy, *refs):
    *parts, out, points, held, here, field, part_sems, in_sems, out_sems, energy_sem = refs
    bins = points.shape[0]
    size = bins // GROUPS
    given = points_copies(parts, points, part_sems)
    for copy in given:
        copy.start()
    energy_copy = pltpu.make_async_copy(energy, held, energy_sem)
    copies = start_rows(mine, here, in_sems, size)
    energy_copy.start()
    for copy in given:
        copy.wait()
    outs = []

    def finish(start):
        at = pl.ds(start, size)
        for row in range(2):
            field[row, at, :] = field[row, at, :] + held[pl.ds(2 * start + row, size, stride=2), :]
        outs.append(pltpu.make_async_copy(field.at[:, at, :], out.at[:, at, :], out_sems.at[len(outs)]))
        outs[-1].start()

    waiting = []
    for j, weights, rows, start in blocks(band_ref[0], here, other, bins):
        if j >= GROUPS - len(copies):
            copies[j - GROUPS + len(copies)].wait()
        src = gained(*dots(weights, rows, points))
        for row in range(2):
            field[row, pl.ds(start, size), :] = src[:, row_cells(row)]
        waiting.append(start)
        if j == GROUPS // 2:
            energy_copy.wait()
        if j >= GROUPS // 2:
            for item in waiting:
                finish(item)
            waiting = []
    for copy in outs:
        copy.wait()


def near_kernel(band_ref, mine, other, own, *refs):
    *parts, late, field, here, own_here, points, late_here, in_sems, own_sem, late_sem = refs
    bins = points.shape[0]
    size = bins // GROUPS
    split = bins - late.shape[1]
    late_copy = pltpu.make_async_copy(late, late_here, late_sem)
    late_copy.start()
    copies = start_rows(mine, here, in_sems, size)
    own_copy = pltpu.make_async_copy(own, own_here, own_sem)
    own_copy.start()
    gather_points(parts, points)
    early = []
    for j, weights, rows, start in blocks(band_ref[0], here, other, bins):
        if j < 2:
            early.append(dots(weights, rows, points.at[:split, :]))
    late_copy.wait()
    gather_points([late_here], points, split)
    for j, weights, rows, start in blocks(band_ref[0], here, other, bins):
        if j >= GROUPS - len(copies):
            copies[j - GROUPS + len(copies)].wait()
        if j < len(early):
            src = gained(*[x + y for x, y in zip(early[j], dots(weights, rows, points.at[split:, :], split))])
        else:
            src = gained(*dots(weights, rows, points))
        at = pl.ds(start, size)
        for row in range(2):
            field[row, at, :] = points[at, row_cells(row)].astype(F32) + src[:, row_cells(row)]
    own_copy.wait()


def inside_points(wide_ref, last, parts, points, start=0):
    w = wide_ref[0]
    inside = (w != 0) & (w != last)

    @pl.when(inside)
    def _():
        gather_points(parts, points, start)

    @pl.when(jnp.logical_not(inside))
    def _():
        size = sum(part.shape[1] for part in parts)
        points[pl.ds(start, size), :] = jnp.zeros((size, points.shape[1]), points.dtype)


def partial_kernel(last, band_ref, wide_ref, mine, other, *refs):
    *parts, sums, points = refs
    bins = sums.shape[1]
    inside_points(wide_ref, last, parts, points)
    for _, weights, rows, at in blocks(band_ref[0], mine, other, bins):
        for i, value in enumerate(dots(weights, rows, points)):
            sums[i, pl.ds(at, value.shape[0]), :] = value


def limited(a, b):
    return jnp.minimum(jnp.maximum(a, jnp.minimum(b, 0.0)), jnp.maximum(b, 0.0))


def row_kernel(last, band_ref, wide_ref, mine, other, sums, courants, own, near, *refs):
    *parts, field, edge, points, far = refs
    bins = points.shape[0]
    first = bins - parts[-1].shape[1]
    size = bins // GROUPS
    odd = lax.rem(wide_ref[0], 2)
    to_right = band_ref[0] == 0
    inside_points(wide_ref, last, parts, points)
    late = points.at[first:, :]
    lane = lax.broadcasted_iota(jnp.int32, (8, 128), 1)
    edge_lane = jnp.where(to_right, 126, 0)

    def sweep(j, weights, rows, start, behind, ahead):
        group = lax.rem((1 - band_ref[0]) * (GROUPS // 2) + j, GROUPS)
        turns = [4 * (group + GROUPS * row) for row in range(2)]
        marks = [((lane - edge_lane - turn) & 127) < 2 for turn in turns]
        at = pl.ds(start, size)
        grow, gate = dots(weights, rows, late, first)
        src = gained(sums[0, at, :] + grow, sums[1, at, :] + gate)
        for row in range(2):
            far[row, at, :] = points[at, row_cells(row)].astype(F32) + src[:, row_cells(row)]
        for i in range(0, size, 8):
            here = pl.ds(pl.multiple_of(start + i, 8), 8)
            c = courants[here, :]
            forward = c >= 0.0
            a = jnp.abs(c)
            k = 0.5 * a * (1.0 - a)
            q0, q1 = own[0, here, :], own[1, here, :]
            m2 = jnp.where(forward, behind[0, here, :], ahead[1, here, :])
            m1 = jnp.where(forward, behind[1, here, :], ahead[0, here, :])
            c0 = jnp.where(forward, q0, q1)
            c1 = jnp.where(forward, q1, q0)
            p2 = jnp.where(forward, ahead[0, here, :], behind[1, here, :])
            da, db, dc, dd = m1 - m2, c0 - m1, c1 - c0, p2 - c1
            fa = a * m1 + k * limited(db, da)
            fb = a * c0 + k * limited(dc, db)
            fc = a * c1 + k * limited(dd, dc)
            n0 = c0 - (fb - fa)
            n1 = c1 - (fc - fb)
            o0 = jnp.where(forward, n0, n1)
            o1 = jnp.where(forward, n1, n0)
            field[0, here, :] = o0
            field[1, here, :] = o1
            folded = edge[i : i + 8, :] if j else jnp.zeros_like(o0)
            for mark, turn, value in zip(marks, turns, (o0, o1)):
                folded = jnp.where(mark, pltpu.roll(value, turn, axis=1), folded)
            edge[i : i + 8, :] = folded

    def run(behind, ahead):
        for j, weights, rows, start in blocks(band_ref[0], mine, other, bins):
            sweep(j, weights, rows, start, behind, ahead)

    @pl.when(odd == 1)
    def _():
        run(near, far)

    @pl.when(odd == 0)
    def _():
        run(far, near)


def col_kernel(wide_ref, courants, sea, field, beside, out, held, sems):
    size = beside.shape[0]
    place = 2 * wide_ref[0]
    lane = lax.broadcasted_iota(jnp.int32, (GROUPS, STEP, 128), 2)
    low, high, first, last = lane < 2, lane >= 126, lane == 0, lane == 127
    mask = [jnp.broadcast_to(sea[pl.ds(place + row, 1), :].astype(F32), (STEP, 128)) for row in range(2)]

    def roll(x, by):
        return pltpu.roll(x, by % 128, axis=2)

    def body(i, carry):
        i = pl.multiple_of(i * STEP, STEP)
        here = pl.ds(i, STEP)
        folded = beside[here, :]
        c = courants[:, here, :]
        forward = c >= 0.0
        a = jnp.abs(c)
        k = 0.5 * a * (1.0 - a)
        halos = [jnp.stack([pltpu.roll(folded, -4 * (group + GROUPS * row) % 128, axis=1)
                            if group + row else folded for group in range(GROUPS)]) for row in range(2)]
        cells = [field[row, :, here, :] for row in range(2)]
        shifted = [(roll(jnp.where(last, halo, q), 1), roll(jnp.where(high, halo, q), 2),
                    roll(jnp.where(first, halo, q), -1), roll(jnp.where(low, halo, q), -2))
                   for halo, q in zip(halos, cells)]
        for row, (q, (l1, l2, r1, r2)) in enumerate(zip(cells, shifted)):
            m2 = jnp.where(forward, l2, r2)
            m1 = jnp.where(forward, l1, r1)
            p1 = jnp.where(forward, r1, l1)
            da, db, dc = m1 - m2, q - m1, p1 - q
            fa = a * m1 + k * limited(db, da)
            fb = a * q + k * limited(dc, db)
            new = (q - (fb - fa)) * mask[row]
            for group in range(GROUPS):
                held[pl.ds(2 * (group * size + i) + row, STEP, stride=2), :] = new[group]
        return carry

    copies = []
    step = size // 3
    for part in range(3):
        lax.fori_loop(part * step // STEP, (part + 1) * step // STEP, body, 0)
        for group in range(GROUPS):
            rows = pl.ds(2 * (group * size + part * step), 2 * step)
            copies.append(pltpu.make_async_copy(held.at[rows, :], out.at[rows, :], sems.at[len(copies)]))
            copies[-1].start()
    for copy in copies:
        copy.wait()


def relay_pairs(count, apart):
    up, down = list(range(0, count, 2)), list(range(count - 1, 0, -2))
    rings = [up, down] if apart else [up + down]
    return [pair for order in rings for pair in zip(order, order[1:] + order[:1])]


def local(energy, source_weights, speed, direction, sea_mask):
    bins, rows, cols = energy.shape
    wide, bands = lax.axis_size("wide"), lax.axis_size("band")
    if rows != 2 or cols != 128 or wide % 2 or bands != 2 or bins % (48 * GROUPS):
        raise ValueError("block shape")
    w_at = lax.axis_index("wide").astype(jnp.int32).reshape(1)
    b_at = lax.axis_index("band").astype(jnp.int32).reshape(1)
    flat = energy.reshape(bins * rows, cols)
    sizes = chunk_sizes(bins)
    swap = [(i, i ^ 1) for i in range(wide)]
    beside = [(i, i ^ 1) for i in range(bands)]

    other = lax.ppermute(source_weights, "band", beside)

    def prepare(start, these):
        total = sum(these)
        return call(
            functools.partial(prepare_kernel, start), 8,
            out_shape=[jax.ShapeDtypeStruct((2, n, cols), BF16) for n in these],
            in_specs=[HBM], out_specs=[VMEM] * len(these),
            scratch_shapes=[pltpu.VMEM((2 * total, cols), F32), pltpu.SemaphoreType.DMA((total // 128,))],
        )(in_hbm(flat))

    parts = prepare(0, sizes[:1]) + prepare(sizes[0], sizes[1:])
    swapped, relayed = [], []
    for part in parts:
        swapped.append(lax.ppermute(part, "wide", swap))
    for i, part in enumerate(swapped):
        relayed.append(lax.ppermute(part, "wide", relay_pairs(wide, i < len(sizes) - 1)))

    full = jax.ShapeDtypeStruct((2, bins, cols), F32)
    sums = jax.ShapeDtypeStruct((2, bins, 2 * cols), F32)
    points = pltpu.VMEM((bins, 2 * cols), BF16)
    n = len(sizes)
    table = jax.ShapeDtypeStruct((bins, cols), F32)
    half = jax.ShapeDtypeStruct(source_weights.shape, BF16)
    here = pltpu.VMEM(source_weights.shape, BF16)
    in_sems = pltpu.SemaphoreType.DMA((GROUPS // 2,))
    mine = in_hbm(source_weights)
    own = in_hbm(call(
        own_kernel, 9, out_shape=pltpu.HBM(full.shape, F32), in_specs=[SMEM, HBM, VMEM, HBM] + [ANY] * n,
        out_specs=HBM,
        scratch_shapes=[points, pltpu.VMEM((2 * bins, cols), F32), here, pltpu.VMEM(full.shape, F32),
                        pltpu.SemaphoreType.DMA((2 * n,)), in_sems, pltpu.SemaphoreType.DMA((GROUPS,)),
                        pltpu.SemaphoreType.DMA],
    )(b_at, mine, other, in_hbm(flat), *parts))
    row_courants, col_courants = call(
        table_kernel, 4, out_shape=[pltpu.HBM(table.shape, F32)] * 2,
        in_specs=[VMEM] * 2, out_specs=[HBM] * 2,
        scratch_shapes=[pltpu.VMEM(table.shape, F32)] * 2 + [pltpu.SemaphoreType.DMA((2,))],
    )(speed.reshape(-1, 128), direction.reshape(-1, 128))
    near, mine, own = call(
        near_kernel, 8, out_shape=[full, half, full],
        in_specs=[SMEM, HBM, VMEM, HBM] + [VMEM] * (n - 1) + [HBM], out_specs=[VMEM] * 3,
        scratch_shapes=[points, pltpu.VMEM((2, sizes[-1], cols), BF16), in_sems,
                        pltpu.SemaphoreType.DMA, pltpu.SemaphoreType.DMA],
    )(b_at, mine, other, own, *swapped[:-1], in_hbm(swapped[-1]))
    early = call(
        functools.partial(partial_kernel, wide - 1), 8, out_shape=sums,
        in_specs=[SMEM, SMEM] + [VMEM] * (1 + n), out_specs=VMEM,
        scratch_shapes=[pltpu.VMEM((bins - sizes[-1], 2 * cols), BF16)],
    )(b_at, w_at, mine, other, *relayed[:-1])
    field, edge = call(
        functools.partial(row_kernel, wide - 1), 10,
        out_shape=[full, jax.ShapeDtypeStruct((bins // GROUPS, cols), F32)],
        in_specs=[SMEM, SMEM] + [VMEM] * (6 + n), out_specs=[VMEM, VMEM],
        scratch_shapes=[points, pltpu.VMEM((2, bins, cols), F32)],
    )(b_at, w_at, mine, other, early, row_courants, own, near, *relayed)
    edges = lax.ppermute(edge, "band", beside)
    out = call(
        col_kernel, 10, out_shape=jax.ShapeDtypeStruct((bins * rows, cols), F32),
        in_specs=[SMEM] + [VMEM] * 4, out_specs=HBM,
        scratch_shapes=[pltpu.VMEM((bins * rows, cols), F32), pltpu.SemaphoreType.DMA((3 * GROUPS,))],
    )(w_at, col_courants.reshape(GROUPS, -1, cols), sea_mask, field.reshape(2, GROUPS, -1, cols), edges)
    return out.reshape(bins, rows, cols)


def solution(mesh):
    return jax.shard_map(
        local,
        mesh=mesh,
        in_specs=(
            P(None, ("grid", "wide"), "band"),
            P(None, "band", None),
            P(),
            P(),
            P("grid", "band"),
        ),
        out_specs=P(None, ("grid", "wide"), "band"),
        check_vma=False,
    )
```

```python
import functools
import math

import jax
import jax.numpy as jnp
from jax import lax
from jax.experimental import pallas as pl
from jax.experimental.pallas import tpu as pltpu
from jax.sharding import PartitionSpec as P

NDIR = 36
TIME_STEP = 0.5
CHUNKS = 2
PIECE = 64
GROUPS = 8
STEP = 16
F32 = jnp.float32
BF16 = jnp.bfloat16
VMEM = pl.BlockSpec(memory_space=pltpu.VMEM)
SMEM = pl.BlockSpec(memory_space=pltpu.SMEM)
HBM = pl.BlockSpec(memory_space=pltpu.HBM)
ANY = pl.BlockSpec(memory_space=pl.ANY)


def call(kernel, mib, **kw):
    return pl.pallas_call(
        kernel,
        compiler_params=pltpu.CompilerParams(vmem_limit_bytes=mib * 1024 * 1024), **kw,
    )


def in_hbm(x):
    return pltpu.with_memory_space_constraint(x, pltpu.HBM)


def chunk_sizes(bins):
    tiles = bins // 64
    cuts = [tiles * i // CHUNKS for i in range(CHUNKS + 1)]
    return [(b - a) * 64 for a, b in zip(cuts, cuts[1:])]


def prepare_kernel(start, energy, *refs):
    *parts, held, sems = refs
    piece = PIECE
    copies = []
    for i in range(held.shape[0] // (2 * piece)):
        from_at, to_at = pl.ds(2 * (start + i * piece), 2 * piece), pl.ds(2 * i * piece, 2 * piece)
        copies.append(pltpu.make_async_copy(energy.at[from_at, :], held.at[to_at, :], sems.at[i]))
        copies[-1].start()
    i = 0
    for part in parts:
        for k in range(0, part.shape[1], piece):
            copies[i].wait()
            for row in range(2):
                part[row, k : k + piece, :] = held[pl.ds(2 * i * piece + row, piece, stride=2), :].astype(BF16)
            i += 1


def points_copies(parts, points, sems):
    copies, start = [], 0
    for part in parts:
        size = part.shape[1]
        for row in range(2):
            target = points.at[pl.ds(start, size), row * 128 : (row + 1) * 128]
            copies.append(pltpu.make_async_copy(part.at[row], target, sems.at[len(copies)]))
        start += size
    return copies


def gather_points(parts, points, start=0):
    for part in parts:
        size = part.shape[1]
        for row in range(2):
            points[pl.ds(start, size), row * 128 : (row + 1) * 128] = part[row]
        start += size


def blocks(band, mine, other, bins):
    size = bins // GROUPS
    half = bins // 2
    for j in range(GROUPS):
        weights, start = (other, (1 - band) * half) if j < GROUPS // 2 else (mine, band * half)
        k = j % (GROUPS // 2) * size
        yield j, weights, slice(k, k + size), pl.multiple_of(start + k, 16)


def dots(weights, rows, points, first=0):
    part = slice(first, first + points.shape[0])
    return [jnp.dot(weights[i, rows, part], points[...], preferred_element_type=F32) for i in range(2)]


def start_rows(source, target, sems, size):
    copies = []
    for j, k in enumerate(range(0, source.shape[1], size)):
        rows = pl.ds(k, size)
        copies.append(pltpu.make_async_copy(source.at[:, rows, :], target.at[:, rows, :], sems.at[j]))
        copies[-1].start()
    return copies


def gained(grow, gate):
    return TIME_STEP * (grow * jax.nn.sigmoid(gate))


def row_cells(row):
    return slice(row * 128, (row + 1) * 128)


def table_kernel(speed, direction, row_out, col_out, row_table, col_table, sems):
    angle = (direction[...].astype(F32) + 0.5) * (2.0 * math.pi / NDIR)
    copies = []
    for n, (out, table, c) in enumerate((
        (row_out, row_table, speed[...] * jnp.sin(angle)), (col_out, col_table, speed[...] * jnp.cos(angle)),
    )):
        turned = c.T
        for r in range(c.shape[0]):
            table[r * 128 : (r + 1) * 128, :] = jnp.broadcast_to(turned[:, r : r + 1], (128, 128))
        copies.append(pltpu.make_async_copy(table, out, sems.at[n]))
        copies[-1].start()
    for copy in copies:
        copy.wait()


def own_kernel(band_ref, mine, other, energy, *refs):
    *parts, out, points, held, here, field, part_sems, in_sems, out_sems, energy_sem = refs
    bins = points.shape[0]
    size = bins // GROUPS
    given = points_copies(parts, points, part_sems)
    for copy in given:
        copy.start()
    energy_copy = pltpu.make_async_copy(energy, held, energy_sem)
    copies = start_rows(mine, here, in_sems, size)
    energy_copy.start()
    for copy in given:
        copy.wait()
    outs = []

    def finish(start):
        at = pl.ds(start, size)
        for row in range(2):
            field[row, at, :] = field[row, at, :] + held[pl.ds(2 * start + row, size, stride=2), :]
        outs.append(pltpu.make_async_copy(field.at[:, at, :], out.at[:, at, :], out_sems.at[len(outs)]))
        outs[-1].start()

    waiting = []
    for j, weights, rows, start in blocks(band_ref[0], here, other, bins):
        if j >= GROUPS - len(copies):
            copies[j - GROUPS + len(copies)].wait()
        src = gained(*dots(weights, rows, points))
        for row in range(2):
            field[row, pl.ds(start, size), :] = src[:, row_cells(row)]
        waiting.append(start)
        if j == GROUPS // 2:
            energy_copy.wait()
        if j >= GROUPS // 2:
            for item in waiting:
                finish(item)
            waiting = []
    for copy in outs:
        copy.wait()


def near_kernel(band_ref, mine, other, own, *refs):
    *parts, late, field, here, own_here, points, late_here, in_sems, own_sem, late_sem = refs
    bins = points.shape[0]
    size = bins // GROUPS
    split = bins - late.shape[1]
    late_copy = pltpu.make_async_copy(late, late_here, late_sem)
    late_copy.start()
    copies = start_rows(mine, here, in_sems, size)
    own_copy = pltpu.make_async_copy(own, own_here, own_sem)
    own_copy.start()
    gather_points(parts, points)
    early = []
    for j, weights, rows, start in blocks(band_ref[0], here, other, bins):
        if j < 2:
            early.append(dots(weights, rows, points.at[:split, :]))
    late_copy.wait()
    gather_points([late_here], points, split)
    for j, weights, rows, start in blocks(band_ref[0], here, other, bins):
        if j >= GROUPS - len(copies):
            copies[j - GROUPS + len(copies)].wait()
        if j < len(early):
            src = gained(*[x + y for x, y in zip(early[j], dots(weights, rows, points.at[split:, :], split))])
        else:
            src = gained(*dots(weights, rows, points))
        at = pl.ds(start, size)
        for row in range(2):
            field[row, at, :] = points[at, row_cells(row)].astype(F32) + src[:, row_cells(row)]
    own_copy.wait()


def inside_points(wide_ref, last, parts, points, start=0):
    w = wide_ref[0]
    inside = (w != 0) & (w != last)

    @pl.when(inside)
    def _():
        gather_points(parts, points, start)

    @pl.when(jnp.logical_not(inside))
    def _():
        size = sum(part.shape[1] for part in parts)
        points[pl.ds(start, size), :] = jnp.zeros((size, points.shape[1]), points.dtype)


def partial_kernel(last, band_ref, wide_ref, mine, other, *refs):
    *parts, sums, points = refs
    bins = sums.shape[1]
    inside_points(wide_ref, last, parts, points)
    for _, weights, rows, at in blocks(band_ref[0], mine, other, bins):
        for i, value in enumerate(dots(weights, rows, points)):
            sums[i, pl.ds(at, value.shape[0]), :] = value


def limited(a, b):
    return jnp.minimum(jnp.maximum(a, jnp.minimum(b, 0.0)), jnp.maximum(b, 0.0))


def row_kernel(last, band_ref, wide_ref, mine, other, sums, courants, own, near, *refs):
    *parts, field, edge, points, far = refs
    bins = points.shape[0]
    first = bins - parts[-1].shape[1]
    size = bins // GROUPS
    odd = lax.rem(wide_ref[0], 2)
    to_right = band_ref[0] == 0
    inside_points(wide_ref, last, parts, points)
    late = points.at[first:, :]
    lane = lax.broadcasted_iota(jnp.int32, (8, 128), 1)
    edge_lane = jnp.where(to_right, 126, 0)

    def sweep(j, weights, rows, start, behind, ahead):
        group = lax.rem((1 - band_ref[0]) * (GROUPS // 2) + j, GROUPS)
        turns = [4 * (group + GROUPS * row) for row in range(2)]
        marks = [((lane - edge_lane - turn) & 127) < 2 for turn in turns]
        at = pl.ds(start, size)
        grow, gate = dots(weights, rows, late, first)
        src = gained(sums[0, at, :] + grow, sums[1, at, :] + gate)
        for row in range(2):
            far[row, at, :] = points[at, row_cells(row)].astype(F32) + src[:, row_cells(row)]
        for i in range(0, size, 8):
            here = pl.ds(pl.multiple_of(start + i, 8), 8)
            c = courants[here, :]
            forward = c >= 0.0
            a = jnp.abs(c)
            k = 0.5 * a * (1.0 - a)
            q0, q1 = own[0, here, :], own[1, here, :]
            m2 = jnp.where(forward, behind[0, here, :], ahead[1, here, :])
            m1 = jnp.where(forward, behind[1, here, :], ahead[0, here, :])
            c0 = jnp.where(forward, q0, q1)
            c1 = jnp.where(forward, q1, q0)
            p2 = jnp.where(forward, ahead[0, here, :], behind[1, here, :])
            da, db, dc, dd = m1 - m2, c0 - m1, c1 - c0, p2 - c1
            fa = a * m1 + k * limited(db, da)
            fb = a * c0 + k * limited(dc, db)
            fc = a * c1 + k * limited(dd, dc)
            n0 = c0 - (fb - fa)
            n1 = c1 - (fc - fb)
            o0 = jnp.where(forward, n0, n1)
            o1 = jnp.where(forward, n1, n0)
            field[0, here, :] = o0
            field[1, here, :] = o1
            folded = edge[i : i + 8, :] if j else jnp.zeros_like(o0)
            for mark, turn, value in zip(marks, turns, (o0, o1)):
                folded = jnp.where(mark, pltpu.roll(value, turn, axis=1), folded)
            edge[i : i + 8, :] = folded

    def run(behind, ahead):
        for j, weights, rows, start in blocks(band_ref[0], mine, other, bins):
            sweep(j, weights, rows, start, behind, ahead)

    @pl.when(odd == 1)
    def _():
        run(near, far)

    @pl.when(odd == 0)
    def _():
        run(far, near)


def col_kernel(wide_ref, courants, sea, field, beside, out, held, sems):
    size = beside.shape[0]
    place = 2 * wide_ref[0]
    lane = lax.broadcasted_iota(jnp.int32, (GROUPS, STEP, 128), 2)
    low, high, first, last = lane < 2, lane >= 126, lane == 0, lane == 127
    mask = [jnp.broadcast_to(sea[pl.ds(place + row, 1), :].astype(F32), (STEP, 128)) for row in range(2)]

    def roll(x, by):
        return pltpu.roll(x, by % 128, axis=2)

    def body(i, carry):
        i = pl.multiple_of(i * STEP, STEP)
        here = pl.ds(i, STEP)
        folded = beside[here, :]
        c = courants[:, here, :]
        forward = c >= 0.0
        a = jnp.abs(c)
        k = 0.5 * a * (1.0 - a)
        halos = [jnp.stack([pltpu.roll(folded, -4 * (group + GROUPS * row) % 128, axis=1)
                            if group + row else folded for group in range(GROUPS)]) for row in range(2)]
        cells = [field[row, :, here, :] for row in range(2)]
        shifted = [(roll(jnp.where(last, halo, q), 1), roll(jnp.where(high, halo, q), 2),
                    roll(jnp.where(first, halo, q), -1), roll(jnp.where(low, halo, q), -2))
                   for halo, q in zip(halos, cells)]
        for row, (q, (l1, l2, r1, r2)) in enumerate(zip(cells, shifted)):
            m2 = jnp.where(forward, l2, r2)
            m1 = jnp.where(forward, l1, r1)
            p1 = jnp.where(forward, r1, l1)
            da, db, dc = m1 - m2, q - m1, p1 - q
            fa = a * m1 + k * limited(db, da)
            fb = a * q + k * limited(dc, db)
            new = (q - (fb - fa)) * mask[row]
            for group in range(GROUPS):
                held[pl.ds(2 * (group * size + i) + row, STEP, stride=2), :] = new[group]
        return carry

    copies = []
    step = size // 3
    for part in range(3):
        lax.fori_loop(part * step // STEP, (part + 1) * step // STEP, body, 0)
        for group in range(GROUPS):
            rows = pl.ds(2 * (group * size + part * step), 2 * step)
            copies.append(pltpu.make_async_copy(held.at[rows, :], out.at[rows, :], sems.at[len(copies)]))
            copies[-1].start()
    for copy in copies:
        copy.wait()


def relay_pairs(count, apart):
    up, down = list(range(0, count, 2)), list(range(count - 1, 0, -2))
    rings = [up, down] if apart else [up + down]
    return [pair for order in rings for pair in zip(order, order[1:] + order[:1])]


def local(energy, source_weights, speed, direction, sea_mask):
    bins, rows, cols = energy.shape
    wide, bands = lax.axis_size("wide"), lax.axis_size("band")
    if rows != 2 or cols != 128 or wide % 2 or bands != 2 or bins % (48 * GROUPS):
        raise ValueError("block shape")
    w_at = lax.axis_index("wide").astype(jnp.int32).reshape(1)
    b_at = lax.axis_index("band").astype(jnp.int32).reshape(1)
    flat = energy.reshape(bins * rows, cols)
    sizes = chunk_sizes(bins)
    swap = [(i, i ^ 1) for i in range(wide)]
    beside = [(i, i ^ 1) for i in range(bands)]

    other = lax.ppermute(source_weights, "band", beside)

    def prepare(start, these):
        total = sum(these)
        return call(
            functools.partial(prepare_kernel, start), 8,
            out_shape=[jax.ShapeDtypeStruct((2, n, cols), BF16) for n in these],
            in_specs=[HBM], out_specs=[VMEM] * len(these),
            scratch_shapes=[pltpu.VMEM((2 * total, cols), F32), pltpu.SemaphoreType.DMA((total // PIECE,))],
        )(in_hbm(flat))

    parts = prepare(0, sizes[:1]) + prepare(sizes[0], sizes[1:])
    swapped, relayed = [], []
    for part in parts:
        swapped.append(lax.ppermute(part, "wide", swap))
    for i, part in enumerate(swapped):
        relayed.append(lax.ppermute(part, "wide", relay_pairs(wide, i < len(sizes) - 1)))

    full = jax.ShapeDtypeStruct((2, bins, cols), F32)
    sums = jax.ShapeDtypeStruct((2, bins, 2 * cols), F32)
    points = pltpu.VMEM((bins, 2 * cols), BF16)
    n = len(sizes)
    table = jax.ShapeDtypeStruct((bins, cols), F32)
    half = jax.ShapeDtypeStruct(source_weights.shape, BF16)
    here = pltpu.VMEM(source_weights.shape, BF16)
    in_sems = pltpu.SemaphoreType.DMA((GROUPS // 2,))
    mine = in_hbm(source_weights)
    own = in_hbm(call(
        own_kernel, 9, out_shape=pltpu.HBM(full.shape, F32), in_specs=[SMEM, HBM, VMEM, HBM] + [ANY] * n,
        out_specs=HBM,
        scratch_shapes=[points, pltpu.VMEM((2 * bins, cols), F32), here, pltpu.VMEM(full.shape, F32),
                        pltpu.SemaphoreType.DMA((2 * n,)), in_sems, pltpu.SemaphoreType.DMA((GROUPS,)),
                        pltpu.SemaphoreType.DMA],
    )(b_at, mine, other, in_hbm(flat), *parts))
    row_courants, col_courants = call(
        table_kernel, 4, out_shape=[pltpu.HBM(table.shape, F32)] * 2,
        in_specs=[VMEM] * 2, out_specs=[HBM] * 2,
        scratch_shapes=[pltpu.VMEM(table.shape, F32)] * 2 + [pltpu.SemaphoreType.DMA((2,))],
    )(speed.reshape(-1, 128), direction.reshape(-1, 128))
    near, mine, own = call(
        near_kernel, 8, out_shape=[full, half, full],
        in_specs=[SMEM, HBM, VMEM, HBM] + [VMEM] * (n - 1) + [HBM], out_specs=[VMEM] * 3,
        scratch_shapes=[points, pltpu.VMEM((2, sizes[-1], cols), BF16), in_sems,
                        pltpu.SemaphoreType.DMA, pltpu.SemaphoreType.DMA],
    )(b_at, mine, other, own, *swapped[:-1], in_hbm(swapped[-1]))
    early = call(
        functools.partial(partial_kernel, wide - 1), 8, out_shape=sums,
        in_specs=[SMEM, SMEM] + [VMEM] * (1 + n), out_specs=VMEM,
        scratch_shapes=[pltpu.VMEM((bins - sizes[-1], 2 * cols), BF16)],
    )(b_at, w_at, mine, other, *relayed[:-1])
    relayed[-1] = pltpu.with_memory_space_constraint(relayed[-1], pltpu.VMEM)
    field, edge = call(
        functools.partial(row_kernel, wide - 1), 10,
        out_shape=[full, jax.ShapeDtypeStruct((bins // GROUPS, cols), F32)],
        in_specs=[SMEM, SMEM] + [VMEM] * (6 + n), out_specs=[VMEM, VMEM],
        scratch_shapes=[points, pltpu.VMEM((2, bins, cols), F32)],
    )(b_at, w_at, mine, other, early, row_courants, own, near, *relayed)
    edges = lax.ppermute(edge, "band", beside)
    out = call(
        col_kernel, 10, out_shape=jax.ShapeDtypeStruct((bins * rows, cols), F32),
        in_specs=[SMEM] + [VMEM] * 4, out_specs=HBM,
        scratch_shapes=[pltpu.VMEM((bins * rows, cols), F32), pltpu.SemaphoreType.DMA((3 * GROUPS,))],
    )(w_at, col_courants.reshape(GROUPS, -1, cols), sea_mask, field.reshape(2, GROUPS, -1, cols), edges)
    return out.reshape(bins, rows, cols)


def solution(mesh):
    return jax.shard_map(
        local,
        mesh=mesh,
        in_specs=(
            P(None, ("grid", "wide"), "band"),
            P(None, "band", None),
            P(),
            P(),
            P("grid", "band"),
        ),
        out_specs=P(None, ("grid", "wide"), "band"),
        check_vma=False,
    )
```

```python
import functools
import math

import jax
import jax.numpy as jnp
from jax import lax
from jax.experimental import pallas as pl
from jax.experimental.pallas import tpu as pltpu
from jax.sharding import PartitionSpec as P

NDIR = 36
TIME_STEP = 0.5
CHUNKS = 2
PIECE = 64
GROUPS = 8
STEP = 16
F32 = jnp.float32
BF16 = jnp.bfloat16
VMEM = pl.BlockSpec(memory_space=pltpu.VMEM)
SMEM = pl.BlockSpec(memory_space=pltpu.SMEM)
HBM = pl.BlockSpec(memory_space=pltpu.HBM)
ANY = pl.BlockSpec(memory_space=pl.ANY)


def call(kernel, mib, **kw):
    return pl.pallas_call(
        kernel,
        compiler_params=pltpu.CompilerParams(vmem_limit_bytes=mib * 1024 * 1024), **kw,
    )


def in_hbm(x):
    return pltpu.with_memory_space_constraint(x, pltpu.HBM)


def chunk_sizes(bins):
    tiles = bins // 64
    cuts = [tiles * i // CHUNKS for i in range(CHUNKS + 1)]
    return [(b - a) * 64 for a, b in zip(cuts, cuts[1:])]


def prepare_kernel(start, energy, *refs):
    *parts, held, sems = refs
    piece = PIECE
    copies = []
    for i in range(held.shape[0] // (2 * piece)):
        from_at, to_at = pl.ds(2 * (start + i * piece), 2 * piece), pl.ds(2 * i * piece, 2 * piece)
        copies.append(pltpu.make_async_copy(energy.at[from_at, :], held.at[to_at, :], sems.at[i]))
        copies[-1].start()
    i = 0
    for part in parts:
        for k in range(0, part.shape[1], piece):
            copies[i].wait()
            for row in range(2):
                part[row, k : k + piece, :] = held[pl.ds(2 * i * piece + row, piece, stride=2), :].astype(BF16)
            i += 1


def points_copies(parts, points, sems):
    copies, start = [], 0
    for part in parts:
        size = part.shape[1]
        for row in range(2):
            target = points.at[pl.ds(start, size), row * 128 : (row + 1) * 128]
            copies.append(pltpu.make_async_copy(part.at[row], target, sems.at[len(copies)]))
        start += size
    return copies


def gather_points(parts, points, start=0):
    for part in parts:
        size = part.shape[1]
        for row in range(2):
            points[pl.ds(start, size), row * 128 : (row + 1) * 128] = part[row]
        start += size


def blocks(band, mine, other, bins):
    size = bins // GROUPS
    half = bins // 2
    for j in range(GROUPS):
        weights, start = (other, (1 - band) * half) if j < GROUPS // 2 else (mine, band * half)
        k = j % (GROUPS // 2) * size
        yield j, weights, slice(k, k + size), pl.multiple_of(start + k, 16)


def dots(weights, rows, points, first=0):
    part = slice(first, first + points.shape[0])
    return [jnp.dot(weights[i, rows, part], points[...], preferred_element_type=F32) for i in range(2)]


def start_rows(source, target, sems, size):
    copies = []
    for j, k in enumerate(range(0, source.shape[1], size)):
        rows = pl.ds(k, size)
        copies.append(pltpu.make_async_copy(source.at[:, rows, :], target.at[:, rows, :], sems.at[j]))
        copies[-1].start()
    return copies


def gained(grow, gate):
    return TIME_STEP * (grow * jax.nn.sigmoid(gate))


def row_cells(row):
    return slice(row * 128, (row + 1) * 128)


def table_kernel(speed, direction, row_out, col_out, row_table, col_table, sems):
    angle = (direction[...].astype(F32) + 0.5) * (2.0 * math.pi / NDIR)
    copies = []
    for n, (out, table, c) in enumerate((
        (row_out, row_table, speed[...] * jnp.sin(angle)), (col_out, col_table, speed[...] * jnp.cos(angle)),
    )):
        turned = c.T
        for r in range(c.shape[0]):
            table[r * 128 : (r + 1) * 128, :] = jnp.broadcast_to(turned[:, r : r + 1], (128, 128))
        copies.append(pltpu.make_async_copy(table, out, sems.at[n]))
        copies[-1].start()
    for copy in copies:
        copy.wait()


def own_kernel(band_ref, mine, other, energy, *refs):
    *parts, out, points, held, here, field, part_sems, in_sems, out_sems, energy_sem = refs
    bins = points.shape[0]
    size = bins // GROUPS
    given = points_copies(parts, points, part_sems)
    for copy in given:
        copy.start()
    energy_copy = pltpu.make_async_copy(energy, held, energy_sem)
    copies = start_rows(mine, here, in_sems, size)
    energy_copy.start()
    for copy in given:
        copy.wait()
    outs = []

    def finish(start):
        at = pl.ds(start, size)
        for row in range(2):
            field[row, at, :] = field[row, at, :] + held[pl.ds(2 * start + row, size, stride=2), :]
        outs.append(pltpu.make_async_copy(field.at[:, at, :], out.at[:, at, :], out_sems.at[len(outs)]))
        outs[-1].start()

    waiting = []
    for j, weights, rows, start in blocks(band_ref[0], here, other, bins):
        if j >= GROUPS - len(copies):
            copies[j - GROUPS + len(copies)].wait()
        src = gained(*dots(weights, rows, points))
        for row in range(2):
            field[row, pl.ds(start, size), :] = src[:, row_cells(row)]
        waiting.append(start)
        if j == GROUPS // 2:
            energy_copy.wait()
        if j >= GROUPS // 2:
            for item in waiting:
                finish(item)
            waiting = []
    for copy in outs:
        copy.wait()


def near_kernel(band_ref, mine, other, own, *refs):
    *parts, late, field, here, own_here, points, late_here, in_sems, own_sem, late_sem = refs
    bins = points.shape[0]
    size = bins // GROUPS
    split = bins - late.shape[1]
    late_copy = pltpu.make_async_copy(late, late_here, late_sem)
    late_copy.start()
    copies = start_rows(mine, here, in_sems, size)
    own_copy = pltpu.make_async_copy(own, own_here, own_sem)
    own_copy.start()
    gather_points(parts, points)
    early = []
    for j, weights, rows, start in blocks(band_ref[0], here, other, bins):
        if j < 2:
            early.append(dots(weights, rows, points.at[:split, :]))
    late_copy.wait()
    gather_points([late_here], points, split)
    for j, weights, rows, start in blocks(band_ref[0], here, other, bins):
        if j >= GROUPS - len(copies):
            copies[j - GROUPS + len(copies)].wait()
        if j < len(early):
            src = gained(*[x + y for x, y in zip(early[j], dots(weights, rows, points.at[split:, :], split))])
        else:
            src = gained(*dots(weights, rows, points))
        at = pl.ds(start, size)
        for row in range(2):
            field[row, at, :] = points[at, row_cells(row)].astype(F32) + src[:, row_cells(row)]
    own_copy.wait()


def inside_points(wide_ref, last, parts, points, start=0):
    w = wide_ref[0]
    inside = (w != 0) & (w != last)

    @pl.when(inside)
    def _():
        gather_points(parts, points, start)

    @pl.when(jnp.logical_not(inside))
    def _():
        size = sum(part.shape[1] for part in parts)
        points[pl.ds(start, size), :] = jnp.zeros((size, points.shape[1]), points.dtype)


def partial_kernel(last, band_ref, wide_ref, mine, other, *refs):
    *parts, sums, points = refs
    bins = sums.shape[1]
    inside_points(wide_ref, last, parts, points)
    for _, weights, rows, at in blocks(band_ref[0], mine, other, bins):
        for i, value in enumerate(dots(weights, rows, points)):
            sums[i, pl.ds(at, value.shape[0]), :] = value


def limited(a, b):
    return jnp.minimum(jnp.maximum(a, jnp.minimum(b, 0.0)), jnp.maximum(b, 0.0))


def row_kernel(last, band_ref, wide_ref, mine, other, sums, courants, own, near, *refs):
    *parts, field, edge, points, far = refs
    bins = points.shape[0]
    first = bins - parts[-1].shape[1]
    size = bins // GROUPS
    odd = lax.rem(wide_ref[0], 2)
    to_right = band_ref[0] == 0
    inside_points(wide_ref, last, parts, points)
    late = points.at[first:, :]
    lane = lax.broadcasted_iota(jnp.int32, (8, 128), 1)
    edge_lane = jnp.where(to_right, 0, 4)

    def sweep(j, weights, rows, start, behind, ahead):
        group = lax.rem((1 - band_ref[0]) * (GROUPS // 2) + j, GROUPS)
        slots = [8 * (group + GROUPS * row) for row in range(2)]
        turns = [slot + 4 & 127 for slot in slots]
        marks = [((lane - edge_lane - slot) & 127) < 4 for slot in slots]
        at = pl.ds(start, size)
        grow, gate = dots(weights, rows, late, first)
        src = gained(sums[0, at, :] + grow, sums[1, at, :] + gate)
        for row in range(2):
            far[row, at, :] = points[at, row_cells(row)].astype(F32) + src[:, row_cells(row)]
        for i in range(0, size, 8):
            here = pl.ds(pl.multiple_of(start + i, 8), 8)
            c = courants[here, :]
            forward = c >= 0.0
            a = jnp.abs(c)
            k = 0.5 * a * (1.0 - a)
            q0, q1 = own[0, here, :], own[1, here, :]
            m2 = jnp.where(forward, behind[0, here, :], ahead[1, here, :])
            m1 = jnp.where(forward, behind[1, here, :], ahead[0, here, :])
            c0 = jnp.where(forward, q0, q1)
            c1 = jnp.where(forward, q1, q0)
            p2 = jnp.where(forward, ahead[0, here, :], behind[1, here, :])
            da, db, dc, dd = m1 - m2, c0 - m1, c1 - c0, p2 - c1
            fa = a * m1 + k * limited(db, da)
            fb = a * c0 + k * limited(dc, db)
            fc = a * c1 + k * limited(dd, dc)
            n0 = c0 - (fb - fa)
            n1 = c1 - (fc - fb)
            o0 = jnp.where(forward, n0, n1)
            o1 = jnp.where(forward, n1, n0)
            field[0, here, :] = o0
            field[1, here, :] = o1
            folded = edge[i : i + 8, :] if j else jnp.zeros_like(o0)
            for mark, turn, value in zip(marks, turns, (o0, o1)):
                folded = jnp.where(mark, pltpu.roll(value, turn, axis=1), folded)
            edge[i : i + 8, :] = folded

    def run(behind, ahead):
        for j, weights, rows, start in blocks(band_ref[0], mine, other, bins):
            sweep(j, weights, rows, start, behind, ahead)

    @pl.when(odd == 1)
    def _():
        run(near, far)

    @pl.when(odd == 0)
    def _():
        run(far, near)


def sea_rows(wide_ref, sea, size):
    place = 2 * wide_ref[0]
    return [jnp.broadcast_to(sea[pl.ds(place + row, 1), :].astype(F32), (size, 128)) for row in range(2)]


def along_lanes(c, q, l1, l2, r1, r2):
    forward = c >= 0.0
    a = jnp.abs(c)
    k = 0.5 * a * (1.0 - a)
    m2 = jnp.where(forward, l2, r2)
    m1 = jnp.where(forward, l1, r1)
    p1 = jnp.where(forward, r1, l1)
    da, db, dc = m1 - m2, q - m1, p1 - q
    fa = a * m1 + k * limited(db, da)
    fb = a * q + k * limited(dc, db)
    return q - (fb - fa)


def col_kernel(wide_ref, courants, sea, field, out):
    lane = lax.broadcasted_iota(jnp.int32, (GROUPS, STEP, 128), 2)
    low, high, first, last = lane < 2, lane >= 126, lane == 0, lane == 127
    mask = sea_rows(wide_ref, sea, STEP)

    def roll(ends, q, by):
        return pltpu.roll(jnp.where(ends, 0.0, q), by % 128, axis=2)

    def body(i, carry):
        here = pl.ds(pl.multiple_of(i * STEP, STEP), STEP)
        c = courants[:, here, :]
        cells = [field[row, :, here, :] for row in range(2)]
        shifted = [(roll(last, q, 1), roll(high, q, 2), roll(first, q, -1), roll(low, q, -2)) for q in cells]
        for row in range(2):
            out[row, :, here, :] = along_lanes(c, cells[row], *shifted[row]) * mask[row]
        return carry

    lax.fori_loop(0, field.shape[2] // STEP, body, 0)


def border_kernel(band_ref, wide_ref, courants, sea, swept, edge, beside, out, held, sems):
    size = edge.shape[0]
    lane = lax.broadcasted_iota(jnp.int32, (size, 128), 1)
    mask = sea_rows(wide_ref, sea, size)
    cells = edge[...] + beside[...]
    c = courants[0]
    for group in range(1, GROUPS):
        c = jnp.where((lane >> 3) % GROUPS == group, courants[group], c)
    new = along_lanes(c, cells, *[pltpu.roll(cells, by % 128, axis=1) for by in (1, 2, -1, -2)])
    border = ((lane + jnp.where(band_ref[0] == 0, 2, 0)) & 127) < 2
    copies = []
    for group in range(GROUPS):
        for row in range(2):
            here = pltpu.roll(new, -(8 * (group + GROUPS * row) + 4) % 128, axis=1)
            value = jnp.where(border, here * mask[row], swept[row, group])
            held[pl.ds(2 * group * size + row, size, stride=2), :] = value
        rows = pl.ds(2 * group * size, 2 * size)
        copies.append(pltpu.make_async_copy(held.at[rows, :], out.at[rows, :], sems.at[group]))
        copies[-1].start()
    for copy in copies:
        copy.wait()


def relay_pairs(count, apart):
    up, down = list(range(0, count, 2)), list(range(count - 1, 0, -2))
    rings = [up, down] if apart else [up + down]
    return [pair for order in rings for pair in zip(order, order[1:] + order[:1])]


def local(energy, source_weights, speed, direction, sea_mask):
    bins, rows, cols = energy.shape
    wide, bands = lax.axis_size("wide"), lax.axis_size("band")
    if rows != 2 or cols != 128 or wide % 2 or bands != 2 or bins % (48 * GROUPS):
        raise ValueError("block shape")
    w_at = lax.axis_index("wide").astype(jnp.int32).reshape(1)
    b_at = lax.axis_index("band").astype(jnp.int32).reshape(1)
    flat = energy.reshape(bins * rows, cols)
    sizes = chunk_sizes(bins)
    swap = [(i, i ^ 1) for i in range(wide)]
    beside = [(i, i ^ 1) for i in range(bands)]

    other = lax.ppermute(source_weights, "band", beside)

    def prepare(start, these):
        total = sum(these)
        return call(
            functools.partial(prepare_kernel, start), 8,
            out_shape=[jax.ShapeDtypeStruct((2, n, cols), BF16) for n in these],
            in_specs=[HBM], out_specs=[VMEM] * len(these),
            scratch_shapes=[pltpu.VMEM((2 * total, cols), F32), pltpu.SemaphoreType.DMA((total // PIECE,))],
        )(in_hbm(flat))

    parts = prepare(0, sizes[:1]) + prepare(sizes[0], sizes[1:])
    swapped, relayed = [], []
    for part in parts:
        swapped.append(lax.ppermute(part, "wide", swap))
    for i, part in enumerate(swapped):
        relayed.append(lax.ppermute(part, "wide", relay_pairs(wide, i < len(sizes) - 1)))

    full = jax.ShapeDtypeStruct((2, bins, cols), F32)
    sums = jax.ShapeDtypeStruct((2, bins, 2 * cols), F32)
    points = pltpu.VMEM((bins, 2 * cols), BF16)
    n = len(sizes)
    table = jax.ShapeDtypeStruct((bins, cols), F32)
    half = jax.ShapeDtypeStruct(source_weights.shape, BF16)
    here = pltpu.VMEM(source_weights.shape, BF16)
    in_sems = pltpu.SemaphoreType.DMA((GROUPS // 2,))
    mine = in_hbm(source_weights)
    own = in_hbm(call(
        own_kernel, 9, out_shape=pltpu.HBM(full.shape, F32), in_specs=[SMEM, HBM, VMEM, HBM] + [ANY] * n,
        out_specs=HBM,
        scratch_shapes=[points, pltpu.VMEM((2 * bins, cols), F32), here, pltpu.VMEM(full.shape, F32),
                        pltpu.SemaphoreType.DMA((2 * n,)), in_sems, pltpu.SemaphoreType.DMA((GROUPS,)),
                        pltpu.SemaphoreType.DMA],
    )(b_at, mine, other, in_hbm(flat), *parts))
    row_courants, col_courants = call(
        table_kernel, 4, out_shape=[pltpu.HBM(table.shape, F32)] * 2,
        in_specs=[VMEM] * 2, out_specs=[HBM] * 2,
        scratch_shapes=[pltpu.VMEM(table.shape, F32)] * 2 + [pltpu.SemaphoreType.DMA((2,))],
    )(speed.reshape(-1, 128), direction.reshape(-1, 128))
    near, mine, own = call(
        near_kernel, 8, out_shape=[full, half, full],
        in_specs=[SMEM, HBM, VMEM, HBM] + [VMEM] * (n - 1) + [HBM], out_specs=[VMEM] * 3,
        scratch_shapes=[points, pltpu.VMEM((2, sizes[-1], cols), BF16), in_sems,
                        pltpu.SemaphoreType.DMA, pltpu.SemaphoreType.DMA],
    )(b_at, mine, other, own, *swapped[:-1], in_hbm(swapped[-1]))
    early = call(
        functools.partial(partial_kernel, wide - 1), 8, out_shape=sums,
        in_specs=[SMEM, SMEM] + [VMEM] * (1 + n), out_specs=VMEM,
        scratch_shapes=[pltpu.VMEM((bins - sizes[-1], 2 * cols), BF16)],
    )(b_at, w_at, mine, other, *relayed[:-1])
    relayed[-1] = pltpu.with_memory_space_constraint(relayed[-1], pltpu.VMEM)
    field, edge = call(
        functools.partial(row_kernel, wide - 1), 10,
        out_shape=[full, jax.ShapeDtypeStruct((bins // GROUPS, cols), F32)],
        in_specs=[SMEM, SMEM] + [VMEM] * (6 + n), out_specs=[VMEM, VMEM],
        scratch_shapes=[points, pltpu.VMEM((2, bins, cols), F32)],
    )(b_at, w_at, mine, other, early, row_courants, own, near, *relayed)
    edges = lax.ppermute(edge, "band", beside)
    grouped = (2, GROUPS, bins // GROUPS, cols)
    col_courants = col_courants.reshape(grouped[1:])
    swept = call(
        col_kernel, 6, out_shape=jax.ShapeDtypeStruct(grouped, F32),
        in_specs=[SMEM] + [VMEM] * 3, out_specs=VMEM,
    )(w_at, col_courants, sea_mask, field.reshape(grouped))
    out = call(
        border_kernel, 6, out_shape=jax.ShapeDtypeStruct((bins * rows, cols), F32),
        in_specs=[SMEM, SMEM] + [VMEM] * 5, out_specs=HBM,
        scratch_shapes=[pltpu.VMEM((bins * rows, cols), F32), pltpu.SemaphoreType.DMA((GROUPS,))],
    )(b_at, w_at, col_courants, sea_mask, swept, edge, edges)
    return out.reshape(bins, rows, cols)


def solution(mesh):
    return jax.shard_map(
        local,
        mesh=mesh,
        in_specs=(
            P(None, ("grid", "wide"), "band"),
            P(None, "band", None),
            P(),
            P(),
            P("grid", "band"),
        ),
        out_specs=P(None, ("grid", "wide"), "band"),
        check_vma=False,
    )
```
